256 devices in a mesh: ia: 4 (over y), ja: 8 (over x, core), ka: 8 (over z).
Axes of the slice: x: 4, y: 4, z: 8, core: 2. Of those that a mesh axis runs over, the one named last changes fastest.
Arguments:
- observed: bfloat16 [4, 8, 40, 128, 32, 128], P('ia', 'ja', 'ka'), may hold values from -6 to 6
- weights: bfloat16 [4, 8, 40, 128, 32, 128], P('ia', 'ja', 'ka'), may hold values from 0 to 4, as said below
- coords: int32 [4, 8, 40, 3], P('ia', 'ja', 'ka'), may hold values from 0 to 31, as said below
- counts: int32 [4, 8, 8], P('ia', 'ja', 'ka'), may hold values from 0 to 5, as said below
- factor_rows: bfloat16 [64, 4096], P(None, ('ia', 'ja', 'ka')), may hold values from -0.75 to 0.75
- factor_cols: bfloat16 [64, 4096], P(None, ('ja', 'ka')), may hold values from -0.75 to 0.75
- factor_depth: bfloat16 [64, 1024], replicated, may hold values from -0.75 to 0.75
- core_tensor: bfloat16 [64, 64, 64], replicated, may hold values from -6 to 6
Outputs:
- rows_gradient: float32 [64, 4096], P(None, ('ia', 'ja', 'ka'))
- cols_gradient: float32 [64, 4096], P(None, ('ja', 'ka'))
- depth_gradient: float32 [64, 1024], P(None, 'ka')
- core_gradient: float32 [64, 64, 64], replicated
The draws below stay inside these ranges and needn't reach their ends.
Inputs may be any that keep to these rules, and one draw needn't show every extreme that they name: counts[a, b, c] is the number of live slots of the device at index a of ia, b of ja, c of ka; the busiest devices hold 5. coords[a, b, c * 5 + s] = (p, q, t) with a * 8 <= p < (a + 1) * 8, b * 4 <= q < (b + 1) * 4, c * 4 <= t < (c + 1) * 4; the 5 slots of one device name distinct blocks. `weights`: zero at unobserved entries, positive at observed ones.
All inputs are finite; a program needn't handle non-finite values.
Results may differ from the reference program's by a relative error of at most 0.0012.
Values may be sent and summed in bfloat16 or wider, within the bound.
A program may use at most 64 MiB of HBM per device.

```python
import math
import jax
import jax.numpy as jnp
from jax import lax

R = 64
BI = 128
BJ = 128
BK = 32
IB_DEV = 8
JB_DEV = 4
KB_DEV = 4
CAP = 5
I = 4096
J = 4096
K = 1024
N_IA = 4
N_JA = 8
N_KA = 8


def draw_weights(key, part):
    full_shape = (N_IA, N_JA, N_KA * CAP, BI, BK, BJ)
    seen_key, level_key = jax.random.split(jax.random.fold_in(key, 7))
    seen_mask = jax.random.bernoulli(seen_key, 0.5, full_shape)
    level_value = jnp.exp(jax.random.uniform(level_key, full_shape, jnp.float32, math.log(0.25), math.log(4.0)))
    return jnp.where(seen_mask, level_value, 0.0).astype(jnp.bfloat16)


def draw_counts(key, part):
    base_key, rare_key, pick_key = jax.random.split(jax.random.fold_in(key, 11), 3)
    full_shape = (N_IA, N_JA, N_KA)
    device_total = N_IA * N_JA * N_KA
    base_count = jax.random.randint(base_key, full_shape, 0, CAP // 2 + 1)
    rare_full = jax.random.randint(rare_key, full_shape, 0, 16) == 0
    chosen = jax.random.randint(pick_key, (), 0, device_total)
    flat_number = jnp.arange(device_total, dtype=jnp.int32).reshape(full_shape)
    full_slots = jnp.logical_or(rare_full, flat_number == chosen)
    return jnp.where(full_slots, CAP, base_count).astype(jnp.int32)


def draw_coords(key, part):
    device_total = N_IA * N_JA * N_KA
    combos = IB_DEV * JB_DEV * KB_DEV
    device_keys = jax.random.split(jax.random.fold_in(key, 23), device_total)
    shuffled = jax.vmap(lambda device_key: jax.random.permutation(device_key, combos))(device_keys)[:, :CAP]
    flat_number = jnp.arange(device_total, dtype=jnp.int32)
    shift_amount = jnp.where(flat_number == device_total - 1, combos - 1 - shuffled[:, 0], 0)
    shift_amount = jnp.where(flat_number == 0, combos - shuffled[:, 0], shift_amount)
    picked = (shuffled + shift_amount[:, None]) % combos
    row_block = picked // (JB_DEV * KB_DEV)
    col_block = picked // KB_DEV % JB_DEV
    depth_block = picked % KB_DEV
    row_owner = flat_number // (N_JA * N_KA)
    col_owner = flat_number // N_KA % N_JA
    depth_owner = flat_number % N_KA
    global_coords = jnp.stack([row_block + row_owner[:, None] * IB_DEV, col_block + col_owner[:, None] * JB_DEV, depth_block + depth_owner[:, None] * KB_DEV], axis=-1)
    return global_coords.reshape(N_IA, N_JA, N_KA * CAP, 3).astype(jnp.int32)


def levels(stream_key, extent, shards, least, high):
    gain, own = 1.0, jax.random.fold_in(stream_key, 6)
    for axis_at, blocks in shards:
        heights = jnp.exp(jax.random.uniform(jax.random.fold_in(own, axis_at), (blocks,), jnp.float32, least / len(shards), high / len(shards)))
        gain = gain * jnp.repeat(heights, extent[axis_at] // blocks).reshape([-1 if axis == axis_at else 1 for axis in range(len(extent))])
    return gain


def normal_values(own_key, extent, scale, reach, cuts=(), kind=jnp.bfloat16):
    factor_of = levels(own_key, extent, cuts, -0.22, 0.18) if cuts else 1.0
    array = jax.random.normal(own_key, extent, jnp.float32) * scale * factor_of
    return jnp.minimum(jnp.maximum(array, -reach), reach).astype(kind)


def setup_inputs(seed: int = 0) -> dict:
    keys = jax.random.split(jax.random.key(seed), 9)
    observed = normal_values(keys[0], (N_IA, N_JA, N_KA * CAP, BI, BK, BJ), 1.0, 6.0, ((0, 4), (1, 8), (2, 8)))
    weights = draw_weights(jax.random.fold_in(keys[8], 71), 0)
    coords = draw_coords(jax.random.fold_in(keys[8], 71), 0)
    counts = draw_counts(jax.random.fold_in(keys[8], 71), 0)
    factor_rows = normal_values(keys[4], (R, I), R ** -0.5, 0.75, ((1, 256),))
    factor_cols = normal_values(keys[5], (R, J), R ** -0.5, 0.75, ((1, 64),))
    factor_depth = normal_values(keys[6], (R, K), R ** -0.5, 0.75)
    core_tensor = normal_values(keys[7], (R, R, R), 1.0, 6.0)
    return {"observed": observed, "weights": weights, "coords": coords, "counts": counts, "factor_rows": factor_rows, "factor_cols": factor_cols, "factor_depth": factor_depth, "core_tensor": core_tensor}


resid_scale = 1.0 / 64.0


def block_terms(observed_block, weight_block, row_factor, col_factor, depth_factor, core_tensor):
    rank_width, block_rows = row_factor.shape
    block_cols = col_factor.shape[1]
    slab_depth = depth_factor.shape[1]
    core_flat = core_tensor.reshape(rank_width * rank_width, rank_width)
    first_cube = jnp.dot(core_flat, depth_factor, preferred_element_type=jnp.float32).astype(jnp.bfloat16)
    first_cube = first_cube.reshape(rank_width, rank_width, slab_depth)
    second_cube = jnp.einsum("rsk,sj->rkj", first_cube.astype(jnp.float32), col_factor.astype(jnp.float32)).astype(jnp.bfloat16)
    second_flat = second_cube.reshape(rank_width, slab_depth * block_cols)
    model_block = jnp.dot(row_factor.T, second_flat, preferred_element_type=jnp.float32)
    weight_flat = weight_block.reshape(block_rows, slab_depth * block_cols).astype(jnp.float32)
    data_flat = observed_block.reshape(block_rows, slab_depth * block_cols).astype(jnp.float32)
    residual = (weight_flat * (model_block - data_flat) * resid_scale).astype(jnp.bfloat16)
    row_term = jnp.dot(second_flat, residual.T, preferred_element_type=jnp.float32)
    first_back = jnp.dot(row_factor, residual, preferred_element_type=jnp.float32).astype(jnp.bfloat16)
    back_cube = first_back.reshape(rank_width, slab_depth, block_cols)
    col_term = jnp.einsum("rsk,rkj->sj", first_cube.astype(jnp.float32), back_cube.astype(jnp.float32))
    second_back = jnp.einsum("sj,rkj->rsk", col_factor.astype(jnp.float32), back_cube.astype(jnp.float32)).astype(jnp.bfloat16)
    back_flat = second_back.reshape(rank_width * rank_width, slab_depth)
    depth_term = jnp.dot(core_flat.T, back_flat, preferred_element_type=jnp.float32)
    core_term = jnp.dot(back_flat, depth_factor.T, preferred_element_type=jnp.float32).reshape(rank_width, rank_width, rank_width)
    return row_term, col_term, depth_term, core_term


def add_columns(table, piece, start_col):
    width = piece.shape[1]
    return lax.dynamic_update_slice_in_dim(table, lax.dynamic_slice_in_dim(table, start_col, width, 1) + piece, start_col, 1)


def reference(observed, weights, coords, counts, factor_rows, factor_cols, factor_depth, core_tensor):
    rank_width = core_tensor.shape[0]
    slot_total = N_IA * N_JA * N_KA * CAP
    data_all = observed.reshape(slot_total, BI, BK, BJ)
    weight_all = weights.reshape(slot_total, BI, BK, BJ)
    coord_all = coords.reshape(slot_total, 3)
    slot_local = jnp.arange(CAP, dtype=jnp.int32)
    live_slot = (slot_local[None, None, None, :] < counts[:, :, :, None]).reshape(slot_total)
    start_sums = (
        jnp.zeros((rank_width, I), jnp.float32),
        jnp.zeros((rank_width, J), jnp.float32),
        jnp.zeros((rank_width, K), jnp.float32),
        jnp.zeros((rank_width, rank_width, rank_width), jnp.float32),
    )

    def accumulate(running, slot_index):
        def add_block(current):
            rows_sum, cols_sum, depth_sum, core_sum = current
            position = coord_all[slot_index]
            row_start = (position[0] * BI).astype(jnp.int32)
            col_start = (position[1] * BJ).astype(jnp.int32)
            depth_start = (position[2] * BK).astype(jnp.int32)
            row_factor = lax.dynamic_slice_in_dim(factor_rows, row_start, BI, 1)
            col_factor = lax.dynamic_slice_in_dim(factor_cols, col_start, BJ, 1)
            depth_factor = lax.dynamic_slice_in_dim(factor_depth, depth_start, BK, 1)
            block_sums = block_terms(data_all[slot_index], weight_all[slot_index], row_factor, col_factor, depth_factor, core_tensor)
            rows_sum = add_columns(rows_sum, block_sums[0], row_start)
            cols_sum = add_columns(cols_sum, block_sums[1], col_start)
            depth_sum = add_columns(depth_sum, block_sums[2], depth_start)
            return (rows_sum, cols_sum, depth_sum, core_sum + block_sums[3])

        def keep_block(current):
            return current

        return lax.cond(live_slot[slot_index], add_block, keep_block, running), None

    finished, _ = lax.scan(accumulate, start_sums, jnp.arange(slot_total, dtype=jnp.int32))
    return (finished[0], finished[1], finished[2], finished[3])
```

```python
import jax
import jax.numpy as jnp
from jax import lax
from jax.experimental import pallas as pl
from jax.experimental.pallas import tpu as pltpu
from jax.sharding import PartitionSpec as P

MESH = pl.DeviceIdType.MESH
f32 = jnp.float32
bf16 = jnp.bfloat16
resid_scale = 1.0 / 64.0

NN = (((1,), (0,)), ((), ()))
NT = (((1,), (1,)), ((), ()))
TN = (((0,), (0,)), ((), ()))


def dot(a, b, dims=NN):
    return lax.dot_general(a, b, dims, preferred_element_type=f32)


def lane_low(shape):
    return lax.broadcasted_iota(jnp.int32, shape, len(shape) - 1) < 64


def two_terms(value):
    lead = value.astype(bf16).astype(f32)
    return jnp.where(lane_low(value.shape), lead, value - lead).astype(bf16)


def unit(size):
    return (
        lax.broadcasted_iota(jnp.int32, (size, size), 0)
        == lax.broadcasted_iota(jnp.int32, (size, size), 1)
    ).astype(bf16)


def gather_kernel(
    rows_ref, cols_ref, depth_ref, core_ref,
    row_out, col_out, slab_out, first_out,
    row_buf, col_buf, first_buf, send_sem, recv_sem,
):
    ja = lax.axis_index("ja")
    ka = lax.axis_index("ka")
    own_rows = rows_ref[...]
    own_cols = cols_ref[...]
    row_buf[ja, pl.ds(pl.multiple_of(ka * 16, 16), 16), :] = dot(
        unit(16), jnp.concatenate([own_rows, own_rows], axis=0), NT
    ).astype(bf16)
    col_buf[ka] = dot(unit(64), jnp.concatenate([own_cols, own_cols], axis=0), NT).astype(bf16)

    barrier = pltpu.get_barrier_semaphore()
    for step in range(1, 8):
        pl.semaphore_signal(barrier, inc=1, device_id={"ka": (ka + step) % 8}, device_id_type=MESH)
        pl.semaphore_signal(barrier, inc=1, device_id={"ja": (ja + step) % 8}, device_id_type=MESH)
    pl.semaphore_wait(barrier, 14)

    def send(ref, slot, target):
        copy = pltpu.make_async_remote_copy(
            src_ref=ref, dst_ref=ref, send_sem=send_sem.at[slot], recv_sem=recv_sem.at[slot],
            device_id=target, device_id_type=MESH,
        )
        copy.start()
        return copy

    own_tile = row_buf.at[ja, pl.ds(pl.multiple_of(ka * 16, 16), 16), :]
    deep_rows = [send(own_tile, step - 1, {"ka": (ka + step) % 8}) for step in range(1, 8)]
    deep_cols = [send(col_buf.at[ka], step + 6, {"ka": (ka + step) % 8}) for step in range(1, 8)]

    slab = depth_ref[:, pl.ds(pl.multiple_of(ka * 128, 128), 128)]
    slab_out[...] = slab
    slab_rows = dot(unit(128), slab, NT).astype(bf16)

    def first_of(r1, carry):
        piece = core_ref[r1]
        first_buf[pl.ds(r1, 128, stride=64), :] = dot(
            slab_rows, jnp.concatenate([piece, piece], axis=0), NT
        )
        return carry

    lax.fori_loop(0, 64, first_of, 0, unroll=8)

    for copy in deep_rows:
        copy.wait_recv()
    wide_rows = [send(row_buf.at[ja], step + 13, {"ja": (ja + step) % 8}) for step in range(1, 8)]

    def round_of(step, carry):
        part = pl.ds(pl.multiple_of(step * 256, 256), 256)
        first_out[part, :] = first_buf[part, :].astype(bf16)
        return carry

    lax.fori_loop(0, 32, round_of, 0, unroll=2)

    for copy in deep_cols:
        copy.wait_recv()
    col_out[...] = col_buf[...]
    for copy in wide_rows:
        copy.wait_recv()
    row_out[...] = row_buf[...]
    for copy in deep_rows + deep_cols + wide_rows:
        copy.wait_send()


def gather_factors(factor_rows, factor_cols, factor_depth, core_tensor):
    vmem = pl.BlockSpec(memory_space=pltpu.VMEM)
    return pl.pallas_call(
        gather_kernel,
        out_shape=(
            jax.ShapeDtypeStruct((8, 128, 128), bf16),
            jax.ShapeDtypeStruct((8, 64, 128), bf16),
            jax.ShapeDtypeStruct((64, 128), bf16),
            jax.ShapeDtypeStruct((8192, 128), bf16),
        ),
        in_specs=[vmem] * 4,
        out_specs=(vmem,) * 4,
        scratch_shapes=[
            pltpu.VMEM((8, 128, 128), bf16),
            pltpu.VMEM((8, 64, 128), bf16),
            pltpu.VMEM((8192, 128), f32),
            pltpu.SemaphoreType.DMA((21,)),
            pltpu.SemaphoreType.DMA((21,)),
        ],
        compiler_params=pltpu.CompilerParams(
            collective_id=0, has_side_effects=True, vmem_limit_bytes=32 << 20
        ),
        name="gather_factors",
    )(factor_rows, factor_cols, factor_depth, core_tensor)


def block_kernel(
    coords, counts,
    data_ref, weight_ref, first_ref, row_ref, col_ref, slab_ref, core_ref,
    core_out, rows_out, cols_out, depth_out,
    mid, back_sum, col_sum,
):
    slot = pl.program_id(0)

    @pl.when(slot == 0)
    def _():
        rows_out[...] = jnp.zeros_like(rows_out)
        back_sum[...] = jnp.zeros_like(back_sum)
        col_sum[...] = jnp.zeros_like(col_sum)

    @pl.when(slot < counts[0])
    def _():
        p = coords[slot * 3] & 7
        q = coords[slot * 3 + 1] & 3
        t = coords[slot * 3 + 2] & 3
        row_t = row_ref[p][:, :64]
        col_t = col_ref[pl.ds(q * 2, 2)].reshape(128, 128)
        row_n = dot(unit(64), row_t, NT).astype(bf16)
        first_base = t * 2048

        def first_pair(pair):
            k = pair * 2
            at = pl.multiple_of(first_base + k * 64, 128)
            both = first_ref[pl.ds(at, 128), :]
            return k, jnp.concatenate([both[:64], both[64:]], axis=1)

        def forward(pair, carry):
            k, pair_first = first_pair(pair)
            part = dot(row_t, pair_first)
            mid[pl.ds(k, 128, stride=32), :] = part[:, :128]
            mid[pl.ds(k + 1, 128, stride=32), :] = part[:, 128:]
            return carry

        lax.fori_loop(0, 16, forward, 0, unroll=4)

        def middle(step, col_part):
            part = pl.ds(pl.multiple_of(step * 256, 256), 256)
            lead_rest = two_terms(mid[part, :])
            model = dot(lead_rest, col_t, NT)
            residual = (
                weight_ref[0, part, :].astype(f32)
                * (model - data_ref[0, part, :].astype(f32))
                * resid_scale
            ).astype(bf16)
            mid[part, :] = dot(residual, col_t)
            return col_part + dot(lead_rest, residual, TN)

        col_part = lax.fori_loop(0, 16, middle, jnp.zeros((128, 128), f32), unroll=4)
        col_sum[q] += col_part[:64] + col_part[64:]

        def backward(pair, row_part):
            k, pair_first = first_pair(pair)
            back = jnp.concatenate(
                [
                    two_terms(mid[pl.ds(k, 128, stride=32), :]),
                    two_terms(mid[pl.ds(k + 1, 128, stride=32), :]),
                ],
                axis=1,
            )
            both = dot(row_n, back)
            for half in range(2):
                piece = both[:, half * 128 : half * 128 + 128]
                piece = piece + pltpu.roll(piece, 64, axis=1)
                piece = jnp.where(lane_low((32, 128)), piece[:32], piece[32:])
                at = pl.multiple_of((t * 32 + k + half) * 32, 32)
                back_sum[pl.ds(at, 32), :] += piece.astype(bf16).astype(f32)
            return row_part + dot(pair_first, back, NT)

        row_part = lax.fori_loop(0, 16, backward, jnp.zeros((64, 128), f32), unroll=4)
        rows_out[p] += row_part

    @pl.when(slot == pl.num_programs(0) - 1)
    def _():
        cols_out[...] = col_sum[...]
        slab = slab_ref[...]
        slab_twice = jnp.concatenate([slab, slab], axis=1)

        def finish(u, depth_part):
            value = back_sum[pl.ds(u, 128, stride=32), :]
            lead = value.astype(bf16)
            rest = (value - lead.astype(f32)).astype(bf16)
            core_out[u] = dot(slab_twice, jnp.concatenate([lead, rest], axis=0))
            piece = jnp.concatenate([core_ref[u], core_ref[u + 32]], axis=0)
            return depth_part + dot(lead, piece) + dot(rest, piece)

        depth_part = lax.fori_loop(0, 32, finish, jnp.zeros((128, 64), f32), unroll=4)
        depth_out[...] = jnp.concatenate(
            [depth_part, jnp.zeros((128, 64), f32)], axis=1
        ).T[:64]


def block_gradients(coords, counts, data, weights, first, rows, cols, slab, core_tensor):
    slots = data.shape[0]

    def live(slot, coords, counts):
        return (jnp.minimum(slot, jnp.maximum(counts[0] - 1, 0)), 0, 0)

    def whole(shape):
        zeros = (0,) * len(shape)
        return pl.BlockSpec(shape, lambda slot, coords, counts: zeros)

    return pl.pallas_call(
        block_kernel,
        out_shape=(
            jax.ShapeDtypeStruct((32, 64, 128), f32),
            jax.ShapeDtypeStruct((8, 64, 128), f32),
            jax.ShapeDtypeStruct((4, 64, 128), f32),
            jax.ShapeDtypeStruct((64, 128), f32),
        ),
        grid_spec=pltpu.PrefetchScalarGridSpec(
            num_scalar_prefetch=2,
            grid=(slots,),
            in_specs=[
                pl.BlockSpec((1, 4096, 128), live),
                pl.BlockSpec((1, 4096, 128), live),
                whole((8192, 128)),
                whole((8, 128, 128)),
                whole((8, 64, 128)),
                whole((64, 128)),
                whole((64, 64, 64)),
            ],
            out_specs=(
                whole((32, 64, 128)),
                whole((8, 64, 128)),
                whole((4, 64, 128)),
                whole((64, 128)),
            ),
            scratch_shapes=[
                pltpu.VMEM((4096, 128), f32),
                pltpu.VMEM((4096, 128), f32),
                pltpu.VMEM((4, 64, 128), f32),
            ],
        ),
        compiler_params=pltpu.CompilerParams(
            dimension_semantics=("arbitrary",), vmem_limit_bytes=48 << 20
        ),
        name="block_gradients",
    )(coords, counts, data, weights, first, rows, cols, slab, core_tensor)


def reduce_kernel(
    core_ref, rows_ref, cols_ref, depth_ref,
    core_out, rows_out, cols_out, depth_out,
    core_pair, core_sum, core_x, core_y, half_x, half_y, end_y, end_x, tile_sum, tile_in, tile_all, core_all,
    rows_pair, rows_sum, rows_x, rows_t, rows_z,
    cols_y, cols_sum, cols_z, cols_all,
    depth_pair, depth_sum, depth_x, depth_one, depth_y, depth_all,
    send_sem, recv_sem,
):
    y = lax.axis_index("ia")
    ja = lax.axis_index("ja")
    z = lax.axis_index("ka")
    x = ja // 2
    c = ja % 2
    o = 1 - c
    low = pl.ds(0, 32)
    high = pl.ds(32, 32)

    barrier = pltpu.get_barrier_semaphore()

    def mate():
        return {"ja": x * 2 + o}

    def on_x(step):
        return {"ja": ((x + step) % 4) * 2 + c}

    def on_y(step):
        return {"ia": (y + step) % 4}

    def on_z(step):
        return {"ka": (z + step) % 8}

    targets = [mate()] + [on_x(s) for s in (1, 2, 3)] + [on_y(s) for s in (1, 2, 3)]
    targets += [on_z(s) for s in range(1, 8)]
    for target in targets:
        pl.semaphore_signal(barrier, inc=1, device_id=target, device_id_type=MESH)
    pl.semaphore_wait(barrier, len(targets))

    started = []

    def send(src, dst, target):
        slot = len(started)
        copy = pltpu.make_async_remote_copy(
            src_ref=src, dst_ref=dst, send_sem=send_sem.at[slot], recv_sem=recv_sem.at[slot],
            device_id=target, device_id_type=MESH,
        )
        copy.start()
        started.append(copy)
        return copy

    def arrived(copies):
        for copy in copies:
            copy.wait_recv()

    core_c0 = send(core_ref.at[o, :, :, low], core_pair.at[:, :, low], mate())
    core_c1 = send(core_ref.at[o, :, :, high], core_pair.at[:, :, high], mate())
    rows_c = send(rows_ref.at[:, o], rows_pair, mate())
    depth_c = send(depth_ref.at[o], depth_pair, mate())
    cols_s1 = [
        send(cols_ref.at[:, pl.ds(pl.multiple_of(((y + s) % 4) * 16, 16), 16), :], cols_y.at[s - 1], on_y(s))
        for s in (1, 2, 3)
    ]

    core_c0.wait_recv()
    core_sum[:, :, low] = core_ref[c, :, :, low] + core_pair[:, :, low]
    core_x0 = [send(core_sum.at[(x + s) % 4, :, low], core_x.at[s - 1], on_x(s)) for s in (1, 2, 3)]
    core_c1.wait_recv()
    core_sum[:, :, high] = core_ref[c, :, :, high] + core_pair[:, :, high]
    core_y1 = [send(core_sum.at[:, (y + s) % 4, high], core_y.at[s - 1], on_y(s)) for s in (1, 2, 3)]
    rows_c.wait_recv()
    rows_sum[...] = rows_ref[:, c] + rows_pair[...]
    rows_s1 = [send(rows_sum.at[(x + s) % 4], rows_x.at[s - 1], on_x(s)) for s in (1, 2, 3)]
    depth_c.wait_recv()
    depth_sum[...] = depth_ref[c] + depth_pair[...]
    depth_s1 = [send(depth_sum.at[(x + s) % 4], depth_x.at[s - 1], on_x(s)) for s in (1, 2, 3)]

    arrived(cols_s1)
    cols_sum[...] = (
        cols_ref[:, pl.ds(pl.multiple_of(y * 16, 16), 16), :] + cols_y[0] + cols_y[1] + cols_y[2]
    )
    cols_s2 = [send(cols_sum.at[((z + s) % 8) // 2], cols_z.at[s - 1], on_z(s)) for s in range(1, 8)]

    arrived(core_x0)
    half_x[...] = core_sum[x, :, low] + core_x[0] + core_x[1] + core_x[2]
    core_y0 = [send(half_x.at[(y + s) % 4], end_y.at[s - 1], on_y(s)) for s in (1, 2, 3)]
    arrived(core_y1)
    half_y[...] = core_sum[:, y, high] + core_y[0] + core_y[1] + core_y[2]
    core_x1 = [send(half_y.at[(x + s) % 4], end_x.at[s - 1], on_x(s)) for s in (1, 2, 3)]

    arrived(rows_s1)
    rows_own = rows_sum[x] + rows_x[0] + rows_x[1] + rows_x[2]
    rows_t[...] = jnp.concatenate([rows_own, jnp.zeros((64, 128), f32)], axis=0).T
    rows_s2 = [
        send(rows_t.at[pl.ds(pl.multiple_of(((z + s) % 8) * 16, 16), 16), :], rows_z.at[s - 1], on_z(s))
        for s in range(1, 8)
    ]
    arrived(depth_s1)
    depth_one[...] = depth_sum[x] + depth_x[0] + depth_x[1] + depth_x[2]
    depth_s2 = [send(depth_one, depth_y.at[s - 1], on_y(s)) for s in (1, 2, 3)]

    arrived(core_y0)
    tile_sum[low] = half_x[y] + end_y[0] + end_y[1] + end_y[2]
    arrived(core_x1)
    tile_sum[high] = half_y[x] + end_x[0] + end_x[1] + end_x[2]
    core_z = [
        send(tile_sum.at[pl.ds(pl.multiple_of(((z + s) % 8) * 8, 8), 8), :], tile_in.at[s - 1], on_z(s))
        for s in range(1, 8)
    ]

    arrived(cols_s2)
    col_total = cols_sum[z // 2]
    for s in range(7):
        col_total = col_total + cols_z[s]
    cols_all[y] = col_total
    cols_s3 = [send(cols_all.at[y], cols_all.at[y], on_y(s)) for s in (1, 2, 3)]
    arrived(depth_s2)
    depth_all[c, x] = depth_one[...] + depth_y[0] + depth_y[1] + depth_y[2]
    depth_s3 = [send(depth_all.at[c, x], depth_all.at[c, x], on_x(s)) for s in (1, 2, 3)]
    arrived(rows_s2)
    row_total = rows_t[pl.ds(pl.multiple_of(z * 16, 16), 16), :]
    for s in range(7):
        row_total = row_total + rows_z[s]
    rows_out[...] = jnp.concatenate([row_total, jnp.zeros((112, 128), f32)], axis=0).T[:64, :16]

    own = pl.ds(pl.multiple_of(z * 8, 8), 8)
    arrived(core_z)
    total = tile_sum[own, :]
    for s in range(7):
        total = total + tile_in[s]
    tile_all[own, :] = total
    core_g = [send(tile_all.at[own, :], tile_all.at[own, :], on_z(s)) for s in range(1, 8)]
    arrived(depth_s3)
    depth_s4 = send(depth_all.at[c], depth_all.at[c], mate())
    arrived(core_g)
    turned = jnp.concatenate([tile_all[...], jnp.zeros((64, 128), f32)], axis=0).T
    core_all[c, x, y] = turned[:64] + pltpu.roll(turned[64:], 64, axis=1)

    back_y0 = [send(core_all.at[c, x, y, low], core_all.at[c, x, y, low], on_y(s)) for s in (1, 2, 3)]
    back_x1 = [send(core_all.at[c, x, y, high], core_all.at[c, x, y, high], on_x(s)) for s in (1, 2, 3)]
    arrived(back_y0)
    back_x0 = [send(core_all.at[c, x, :, low], core_all.at[c, x, :, low], on_x(s)) for s in (1, 2, 3)]
    arrived(back_x1)
    back_y1 = [send(core_all.at[c, :, y, high], core_all.at[c, :, y, high], on_y(s)) for s in (1, 2, 3)]

    arrived(cols_s3)
    whole = cols_all[...].reshape(64, 128)
    cols_out[...] = jnp.where(z % 2 == 1, pltpu.roll(whole, 64, axis=1), whole)[:, :64]

    arrived(back_x0)
    back_c0 = send(core_all.at[c, :, :, low], core_all.at[c, :, :, low], mate())
    arrived(back_y1)
    back_c1 = send(core_all.at[c, :, :, high], core_all.at[c, :, :, high], mate())
    depth_s4.wait_recv()
    depth_out[...] = depth_all[...].reshape(64, 128)
    core_out[c] = core_all[c]
    back_c0.wait_recv()
    back_c1.wait_recv()
    core_out[o] = core_all[o]
    for copy in started:
        copy.wait_send()


def reduce_gradients(core, rows, cols, depth):
    vmem = pl.BlockSpec(memory_space=pltpu.VMEM)
    copies = 95

    def buf(*shape):
        return pltpu.VMEM(shape, f32)

    return pl.pallas_call(
        reduce_kernel,
        out_shape=(
            jax.ShapeDtypeStruct((2, 4, 4, 64, 128), f32),
            jax.ShapeDtypeStruct((64, 16), f32),
            jax.ShapeDtypeStruct((64, 64), f32),
            jax.ShapeDtypeStruct((64, 128), f32),
        ),
        in_specs=[vmem] * 4,
        out_specs=(vmem,) * 4,
        scratch_shapes=[
            buf(4, 4, 64, 128),
            buf(4, 4, 64, 128),
            buf(3, 4, 32, 128),
            buf(3, 4, 32, 128),
            buf(4, 32, 128),
            buf(4, 32, 128),
            buf(3, 32, 128),
            buf(3, 32, 128),
            buf(64, 128),
            buf(7, 8, 128),
            buf(64, 128),
            buf(2, 4, 4, 64, 128),
            buf(4, 64, 128),
            buf(4, 64, 128),
            buf(3, 64, 128),
            buf(128, 128),
            buf(7, 16, 128),
            buf(3, 4, 16, 128),
            buf(4, 16, 128),
            buf(7, 16, 128),
            buf(4, 16, 128),
            buf(4, 8, 128),
            buf(4, 8, 128),
            buf(3, 8, 128),
            buf(8, 128),
            buf(3, 8, 128),
            buf(2, 4, 8, 128),
            pltpu.SemaphoreType.DMA((copies,)),
            pltpu.SemaphoreType.DMA((copies,)),
        ],
        compiler_params=pltpu.CompilerParams(
            collective_id=1, has_side_effects=True, vmem_limit_bytes=32 << 20
        ),
        name="reduce_gradients",
    )(core, rows, cols, depth)


def on_device(
    observed, weights, coords, counts, factor_rows, factor_cols, factor_depth, core_tensor
):
    slots = observed.shape[2]
    data = observed.reshape(slots, 4096, 128)
    weight = weights.reshape(slots, 4096, 128)
    rows, cols, slab, first = gather_factors(factor_rows, factor_cols, factor_depth, core_tensor)
    core_part, rows_part, cols_part, depth_part = block_gradients(
        coords.reshape(slots * 3), counts.reshape(1), data, weight, first, rows, cols, slab, core_tensor
    )
    core, rows_gradient, cols_gradient, depth_gradient = reduce_gradients(
        core_part.reshape(2, 4, 4, 64, 128),
        rows_part.reshape(4, 2, 64, 128),
        cols_part,
        depth_part.reshape(2, 4, 8, 128),
    )
    core = core.reshape(32, 64, 128)
    core_gradient = jnp.concatenate([core[:, :, :64], core[:, :, 64:]], axis=0)
    return (rows_gradient, cols_gradient, depth_gradient, core_gradient)


def solution(mesh):
    in_specs = (
        P("ia", "ja", "ka", None, None, None),
        P("ia", "ja", "ka", None, None, None),
        P("ia", "ja", "ka", None),
        P("ia", "ja", "ka"),
        P(None, ("ia", "ja", "ka")),
        P(None, ("ja", "ka")),
        P(),
        P(),
    )
    out_specs = (P(None, ("ia", "ja", "ka")), P(None, ("ja", "ka")), P(None, "ka"), P())
    return jax.shard_map(
        on_device, mesh=mesh, in_specs=in_specs, out_specs=out_specs, check_vma=False
    )
```

```python
import jax
import jax.numpy as jnp
from jax import lax
from jax.experimental import pallas as pl
from jax.experimental.pallas import tpu as pltpu
from jax.sharding import PartitionSpec as P

MESH = pl.DeviceIdType.MESH
f32 = jnp.float32
bf16 = jnp.bfloat16
resid_scale = 1.0 / 64.0

NN = (((1,), (0,)), ((), ()))
NT = (((1,), (1,)), ((), ()))
TN = (((0,), (0,)), ((), ()))


def dot(a, b, dims=NN):
    return lax.dot_general(a, b, dims, preferred_element_type=f32)


def low_lanes(shape):
    return lax.broadcasted_iota(jnp.int32, shape, len(shape) - 1) < 64


def unit(size):
    return (
        lax.broadcasted_iota(jnp.int32, (size, size), 0)
        == lax.broadcasted_iota(jnp.int32, (size, size), 1)
    ).astype(bf16)


def twice(value, axis):
    return jnp.concatenate([value, value], axis=axis)


def split_terms(value):
    lead = value.astype(bf16)
    return lead, (value - lead.astype(f32)).astype(bf16)


def half_first(value):
    return jnp.concatenate(
        [value[t * 32 + half * 16 : t * 32 + half * 16 + 16] for half in range(2) for t in range(4)], axis=0
    )


def half_inside(value):
    return jnp.concatenate(
        [value[half * 64 + t * 16 : half * 64 + t * 16 + 16] for t in range(4) for half in range(2)], axis=0
    )


def gather_kernel(
    rows_ref, cols_ref, depth_hbm, core_hbm,
    row_out, col_out, slab_out, first_out,
    row_buf, col_buf, first_buf, slab_in, core_in, send_sem, recv_sem, local_sem,
):
    ja = lax.axis_index("ja")
    ka = lax.axis_index("ka")
    core_copy = pltpu.make_async_copy(core_hbm, core_in, local_sem.at[0])
    core_copy.start()
    slab_copy = pltpu.make_async_copy(
        depth_hbm.at[:, pl.ds(pl.multiple_of(ka * 128, 128), 128)], slab_in, local_sem.at[1]
    )
    slab_copy.start()

    barrier = pltpu.get_barrier_semaphore()
    for step in range(1, 8):
        pl.semaphore_signal(barrier, inc=1, device_id={"ka": (ka + step) % 8}, device_id_type=MESH)
        pl.semaphore_signal(barrier, inc=1, device_id={"ja": (ja + step) % 8}, device_id_type=MESH)

    own_rows = dot(rows_ref[...], twice(unit(64), 1))
    row_buf[ja, ka] = jnp.where(low_lanes((8, 128)), own_rows[:8], own_rows[8:]).astype(bf16)
    own_cols = dot(unit(64), twice(cols_ref[...], 0), NT)
    col_buf[ka] = jnp.where(low_lanes((32, 128)), own_cols[:32], own_cols[32:]).astype(bf16)
    pl.semaphore_wait(barrier, 14)

    def send(ref, slot, target):
        copy = pltpu.make_async_remote_copy(
            src_ref=ref, dst_ref=ref, send_sem=send_sem.at[slot], recv_sem=recv_sem.at[slot],
            device_id=target, device_id_type=MESH,
        )
        copy.start()
        return copy

    order = (4, 3, 5, 2, 6, 1, 7)
    deep_rows = [send(row_buf.at[ja, ka], step - 1, {"ka": (ka + step) % 8}) for step in order]
    deep_cols = [send(col_buf.at[ka], step + 6, {"ka": (ka + step) % 8}) for step in order]

    slab_copy.wait()
    slab_rows = half_first(dot(unit(128), slab_in[...], NT).astype(bf16))
    slab_out[...] = dot(unit(64), slab_rows, NT).astype(bf16)
    core_copy.wait()

    def first_of(pair, carry):
        left = core_in[pair * 2]
        right = core_in[pair * 2 + 1]
        both = dot(slab_rows, jnp.concatenate([left, left, right, right], axis=0), NT)
        for side in range(2):
            piece = both[:, side * 128 : side * 128 + 128]
            first_buf[pl.ds(pair * 2 + side, 64, stride=65), :] = jnp.where(
                low_lanes((64, 128)), piece[:64], piece[64:]
            )
        return carry

    lax.fori_loop(0, 32, first_of, 0, unroll=4)

    for copy in deep_rows:
        copy.wait_recv()
    wide_rows = [send(row_buf.at[ja], step + 13, {"ja": (ja + step) % 8}) for step in order]

    def round_of(step, carry):
        first_out[step] = first_buf[pl.ds(step * 65, 64), :].astype(bf16)
        return carry

    lax.fori_loop(0, 64, round_of, 0, unroll=8)

    for copy in deep_cols:
        copy.wait_recv()
    col_out[...] = col_buf[...]
    for copy in wide_rows:
        copy.wait_recv()
    row_out[...] = row_buf[...]
    for copy in deep_rows + deep_cols + wide_rows:
        copy.wait_send()


def gather_factors(factor_rows, factor_cols, factor_depth, core_tensor):
    vmem = pl.BlockSpec(memory_space=pltpu.VMEM)
    hbm = pl.BlockSpec(memory_space=pltpu.HBM)
    return pl.pallas_call(
        gather_kernel,
        out_shape=(
            jax.ShapeDtypeStruct((8, 8, 8, 128), bf16),
            jax.ShapeDtypeStruct((8, 32, 128), bf16),
            jax.ShapeDtypeStruct((64, 128), bf16),
            jax.ShapeDtypeStruct((64, 64, 128), bf16),
        ),
        in_specs=[vmem, vmem, hbm, hbm],
        out_specs=(vmem,) * 4,
        scratch_shapes=[
            pltpu.VMEM((8, 8, 8, 128), bf16),
            pltpu.VMEM((8, 32, 128), bf16),
            pltpu.VMEM((64 * 65, 128), f32),
            pltpu.VMEM((64, 128), bf16),
            pltpu.VMEM((64, 64, 64), bf16),
            pltpu.SemaphoreType.DMA((21,)),
            pltpu.SemaphoreType.DMA((21,)),
            pltpu.SemaphoreType.DMA((2,)),
        ],
        compiler_params=pltpu.CompilerParams(
            collective_id=0, has_side_effects=True, vmem_limit_bytes=33554432
        ),
        name="gather_factors",
    )(factor_rows, factor_cols, factor_depth, core_tensor)


def block_kernel(
    coords, counts,
    data_ref, weight_ref, first_ref, row_ref, col_ref, slab_ref, core_hbm,
    core_out, rows_out, cols_out, depth_out,
    mid, back_sum, col_sum, core_in, core_sem,
):
    slot = pl.program_id(0)
    last = pl.num_programs(0) - 1

    def core_copy():
        return pltpu.make_async_copy(core_hbm, core_in, core_sem)

    @pl.when(slot == 0)
    def _():
        core_copy().start()
        rows_out[...] = jnp.zeros_like(rows_out)
        back_sum[...] = jnp.zeros_like(back_sum)
        col_sum[...] = jnp.zeros_like(col_sum)

    @pl.when(slot < counts[0, 0, 0])
    def _():
        p = coords[0, 0, slot, 0] & 7
        q = coords[0, 0, slot, 1] & 3
        t = coords[0, 0, slot, 2] & 3
        packed_rows = row_ref[p].astype(f32).reshape(64, 128)
        turned_rows = pltpu.roll(packed_rows, 64, axis=1)
        row_t = jnp.concatenate(
            [part[z * 8 : z * 8 + 8] for z in range(8) for part in (packed_rows, turned_rows)], axis=0
        )[:, :64].astype(bf16)
        row_n = dot(unit(64), row_t, NT).astype(bf16)
        row_n2 = twice(row_n, 1)
        packed_cols = col_ref[pl.ds(q * 2, 2)].astype(f32).reshape(64, 128)
        turned_cols = pltpu.roll(packed_cols, 64, axis=1)
        low = low_lanes((64, 128))
        first_half = jnp.where(low, packed_cols, turned_cols)
        second_half = jnp.where(low, turned_cols, packed_cols)
        col_t = jnp.concatenate(
            [first_half[:32], second_half[:32], first_half[32:], second_half[32:]], axis=0
        )
        low = low_lanes((128, 128))
        zero = jnp.zeros((128, 128), f32)
        col_low = jnp.where(low, col_t, zero)
        col_high = jnp.where(low, zero, col_t)
        to_model = jnp.concatenate([twice(col_low, 1), twice(col_high, 1)], axis=0).astype(bf16)
        to_back = (jnp.concatenate([col_low, col_high], axis=0) * resid_scale).astype(bf16)

        def forward(pair, carry):
            kk = pair * 2
            part = dot(
                row_t, jnp.concatenate([first_ref[t * 16 + kk], first_ref[t * 16 + kk + 1]], axis=1)
            )
            mid[pl.ds(kk, 128, stride=17), :] = part[:, :128]
            mid[pl.ds(kk + 1, 128, stride=17), :] = part[:, 128:]
            return carry

        lax.fori_loop(0, 8, forward, 0, unroll=FORWARD)

        def middle(step, col_part):
            base = step * 16
            lead, rest = split_terms(
                jnp.concatenate([mid[pl.ds((base + i) * 17, 16), :] for i in range(16)], axis=0)
            )
            model = dot(jnp.concatenate([lead, rest], axis=1), to_model, NT)

            def half_of(half):
                at = (0, pl.ds(base, 16), pl.ds(half * 16, 16), slice(None))
                data = data_ref[at].reshape(256, 128).astype(f32)
                weight = weight_ref[at].reshape(256, 128).astype(f32)
                return (weight * (model[:, half * 128 : half * 128 + 128] - data)).astype(bf16)

            residual = jnp.concatenate([half_of(0), half_of(1)], axis=1)
            back = dot(residual, to_back)
            for i in range(16):
                mid[pl.ds((base + i) * 17, 16), :] = back[i * 16 : i * 16 + 16]
            return col_part + dot(lead, residual, TN)

        col_part = lax.fori_loop(0, 8, middle, jnp.zeros((128, 256), f32), unroll=MIDDLE)
        col_sum[q] += (col_part[:64, :128] + col_part[64:, 128:]) * resid_scale

        def backward(kk, row_part):
            lead, rest = split_terms(mid[pl.ds(kk, 128, stride=17), :])
            both = dot(row_n2, jnp.concatenate([lead, rest], axis=0))
            at = pl.ds((t * 16 + kk) * 65, 64)
            back_sum[at, :] += both.astype(bf16).astype(f32)
            return row_part + dot(
                twice(first_ref[t * 16 + kk], 1), jnp.concatenate([lead, rest], axis=1), NT
            )

        row_part = lax.fori_loop(0, 16, backward, jnp.zeros((64, 128), f32), unroll=BACKWARD)
        rows_out[p] += row_part

    @pl.when(slot == last)
    def _():
        cols_out[...] = col_sum[...]
        slab_twice = twice(slab_ref[...], 1)
        core_copy().wait()

        def finish(u, depth_part):
            one = back_sum[pl.ds(u, 64, stride=65), :]
            two = back_sum[pl.ds(u + 32, 64, stride=65), :]
            low = low_lanes((64, 128))
            lead, rest = split_terms(
                jnp.concatenate(
                    [
                        jnp.where(low, one, pltpu.roll(two, 64, axis=1)),
                        jnp.where(low, pltpu.roll(one, 64, axis=1), two),
                    ],
                    axis=0,
                )
            )
            core_out[u] = dot(slab_twice, jnp.concatenate([lead, rest], axis=0))
            piece = jnp.concatenate([core_in[u], core_in[u + 32]], axis=0)
            return depth_part + dot(jnp.concatenate([lead, rest], axis=1), twice(piece, 0))

        depth_part = half_inside(
            lax.fori_loop(0, 32, finish, jnp.zeros((128, 64), f32), unroll=FINISH)
        )
        depth_out[...] = jnp.concatenate(
            [depth_part, jnp.zeros((128, 64), f32)], axis=1
        ).T[:64]


FORWARD, MIDDLE, BACKWARD, FINISH = 4, 2, 4, 4


def block_gradients(coords, counts, data, weights, first, rows, cols, slab, core_tensor):
    slots = data.shape[0]

    def live(slot, coords, counts):
        return (jnp.minimum(slot, jnp.maximum(counts[0, 0, 0] - 1, 0)), 0, 0, 0)

    def whole(shape):
        zeros = (0,) * len(shape)
        return pl.BlockSpec(shape, lambda slot, coords, counts: zeros)

    return pl.pallas_call(
        block_kernel,
        out_shape=(
            jax.ShapeDtypeStruct((32, 64, 128), f32),
            jax.ShapeDtypeStruct((8, 64, 128), f32),
            jax.ShapeDtypeStruct((4, 64, 128), f32),
            jax.ShapeDtypeStruct((64, 128), f32),
        ),
        grid_spec=pltpu.PrefetchScalarGridSpec(
            num_scalar_prefetch=2,
            grid=(slots,),
            in_specs=[
                pl.BlockSpec((1, 128, 32, 128), live),
                pl.BlockSpec((1, 128, 32, 128), live),
                whole((64, 64, 128)),
                whole((8, 8, 8, 128)),
                whole((8, 32, 128)),
                whole((64, 128)),
                pl.BlockSpec(memory_space=pltpu.HBM),
            ],
            out_specs=(
                whole((32, 64, 128)),
                whole((8, 64, 128)),
                whole((4, 64, 128)),
                whole((64, 128)),
            ),
            scratch_shapes=[
                pltpu.VMEM((128 * 17, 128), f32),
                pltpu.VMEM((64 * 65, 128), f32),
                pltpu.VMEM((4, 64, 128), f32),
                pltpu.VMEM((64, 64, 64), bf16),
                pltpu.SemaphoreType.DMA,
            ],
        ),
        compiler_params=pltpu.CompilerParams(
            dimension_semantics=("arbitrary",), vmem_limit_bytes=50331648
        ),
        name="block_gradients",
    )(coords, counts, data, weights, first, rows, cols, slab, core_tensor)


def reduce_kernel(
    core_ref, rows_ref, cols_ref, depth_ref,
    core_out, rows_out, cols_out, depth_out,
    core_pair, core_sum, core_x, core_y, half_x, half_y, end_y, end_x, tile_sum, tile_in, tile_all, core_all,
    rows_pair, rows_sum, rows_x, rows_t, rows_z,
    cols_y, cols_sum, cols_z, cols_all,
    depth_pair, depth_sum, depth_x, depth_one, depth_y, depth_all,
    send_sem, recv_sem,
):
    y = lax.axis_index("ia")
    ja = lax.axis_index("ja")
    z = lax.axis_index("ka")
    x = ja // 2
    c = ja % 2
    o = 1 - c
    low = pl.ds(0, 32)
    high = pl.ds(32, 32)

    barrier = pltpu.get_barrier_semaphore()

    def mate():
        return {"ja": x * 2 + o}

    def on_x(step):
        return {"ja": ((x + step) % 4) * 2 + c}

    def on_y(step):
        return {"ia": (y + step) % 4}

    def on_z(step):
        return {"ka": (z + step) % 8}

    targets = [mate()] + [on_x(s) for s in (1, 2, 3)] + [on_y(s) for s in (1, 2, 3)]
    targets += [on_z(s) for s in range(1, 8)]
    for target in targets:
        pl.semaphore_signal(barrier, inc=1, device_id=target, device_id_type=MESH)
    pl.semaphore_wait(barrier, len(targets))

    started = []

    def send(src, dst, target):
        slot = len(started)
        copy = pltpu.make_async_remote_copy(
            src_ref=src, dst_ref=dst, send_sem=send_sem.at[slot], recv_sem=recv_sem.at[slot],
            device_id=target, device_id_type=MESH,
        )
        copy.start()
        started.append(copy)
        return copy

    def arrived(copies):
        for copy in copies:
            copy.wait_recv()

    core_c0 = send(core_ref.at[o, :, :, low], core_pair.at[:, :, low], mate())
    core_c1 = send(core_ref.at[o, :, :, high], core_pair.at[:, :, high], mate())
    rows_c = send(rows_ref.at[:, o], rows_pair, mate())
    depth_c = send(depth_ref.at[o], depth_pair, mate())
    cols_s1 = [
        send(cols_ref.at[:, pl.ds(pl.multiple_of(((y + s) % 4) * 16, 16), 16), :], cols_y.at[s - 1], on_y(s))
        for s in (1, 2, 3)
    ]

    core_c0.wait_recv()
    core_sum[:, :, low] = core_ref[c, :, :, low] + core_pair[:, :, low]
    core_x0 = [send(core_sum.at[(x + s) % 4, :, low], core_x.at[s - 1], on_x(s)) for s in (1, 2, 3)]
    core_c1.wait_recv()
    core_sum[:, :, high] = core_ref[c, :, :, high] + core_pair[:, :, high]
    core_y1 = [send(core_sum.at[:, (y + s) % 4, high], core_y.at[s - 1], on_y(s)) for s in (1, 2, 3)]
    rows_c.wait_recv()
    rows_sum[...] = rows_ref[:, c] + rows_pair[...]
    rows_s1 = [send(rows_sum.at[(x + s) % 4], rows_x.at[s - 1], on_x(s)) for s in (1, 2, 3)]
    depth_c.wait_recv()
    depth_sum[...] = depth_ref[c] + depth_pair[...]
    depth_s1 = [send(depth_sum.at[(x + s) % 4], depth_x.at[s - 1], on_x(s)) for s in (1, 2, 3)]

    arrived(cols_s1)
    cols_sum[...] = (
        cols_ref[:, pl.ds(pl.multiple_of(y * 16, 16), 16), :] + cols_y[0] + cols_y[1] + cols_y[2]
    )
    cols_s2 = [send(cols_sum.at[((z + s) % 8) // 2], cols_z.at[s - 1], on_z(s)) for s in range(1, 8)]

    arrived(core_x0)
    half_x[...] = core_sum[x, :, low] + core_x[0] + core_x[1] + core_x[2]
    core_y0 = [send(half_x.at[(y + s) % 4], end_y.at[s - 1], on_y(s)) for s in (1, 2, 3)]
    arrived(core_y1)
    half_y[...] = core_sum[:, y, high] + core_y[0] + core_y[1] + core_y[2]
    core_x1 = [send(half_y.at[(x + s) % 4], end_x.at[s - 1], on_x(s)) for s in (1, 2, 3)]

    arrived(rows_s1)
    rows_own = rows_sum[x] + rows_x[0] + rows_x[1] + rows_x[2]
    rows_t[...] = jnp.concatenate([rows_own, jnp.zeros((64, 128), f32)], axis=0).T
    rows_s2 = [
        send(rows_t.at[pl.ds(pl.multiple_of(((z + s) % 8) * 16, 16), 16), :], rows_z.at[s - 1], on_z(s))
        for s in range(1, 8)
    ]
    arrived(depth_s1)
    depth_one[...] = depth_sum[x] + depth_x[0] + depth_x[1] + depth_x[2]
    depth_s2 = [send(depth_one, depth_y.at[s - 1], on_y(s)) for s in (1, 2, 3)]

    arrived(core_y0)
    tile_sum[low] = half_x[y] + end_y[0] + end_y[1] + end_y[2]
    arrived(core_x1)
    tile_sum[high] = half_y[x] + end_x[0] + end_x[1] + end_x[2]
    core_z = [
        send(tile_sum.at[pl.ds(pl.multiple_of(((z + s) % 8) * 8, 8), 8), :], tile_in.at[s - 1], on_z(s))
        for s in range(1, 8)
    ]

    arrived(cols_s2)
    col_total = cols_sum[z // 2]
    for s in range(7):
        col_total = col_total + cols_z[s]
    cols_all[y] = col_total
    cols_s3 = [send(cols_all.at[y], cols_all.at[y], on_y(s)) for s in (1, 2, 3)]
    arrived(depth_s2)
    depth_all[c, x] = depth_one[...] + depth_y[0] + depth_y[1] + depth_y[2]
    depth_s3 = [send(depth_all.at[c, x], depth_all.at[c, x], on_x(s)) for s in (1, 2, 3)]
    arrived(rows_s2)
    row_total = rows_t[pl.ds(pl.multiple_of(z * 16, 16), 16), :]
    for s in range(7):
        row_total = row_total + rows_z[s]
    rows_out[...] = row_total[:, :64]

    own = pl.ds(pl.multiple_of(z * 8, 8), 8)
    arrived(core_z)
    total = tile_sum[own, :]
    for s in range(7):
        total = total + tile_in[s]
    tile_all[own, :] = total
    core_g = [send(tile_all.at[own, :], tile_all.at[own, :], on_z(s)) for s in range(1, 8)]
    arrived(depth_s3)
    depth_s4 = send(depth_all.at[c], depth_all.at[c], mate())
    arrived(core_g)
    turned = jnp.concatenate([tile_all[...], jnp.zeros((64, 128), f32)], axis=0).T
    core_all[c, x, y] = turned[:64] + pltpu.roll(turned[64:], 64, axis=1)

    back_y0 = [send(core_all.at[c, x, y, low], core_all.at[c, x, y, low], on_y(s)) for s in (1, 2, 3)]
    back_x1 = [send(core_all.at[c, x, y, high], core_all.at[c, x, y, high], on_x(s)) for s in (1, 2, 3)]
    arrived(back_y0)
    back_x0 = [send(core_all.at[c, x, :, low], core_all.at[c, x, :, low], on_x(s)) for s in (1, 2, 3)]
    arrived(back_x1)
    back_y1 = [send(core_all.at[c, :, y, high], core_all.at[c, :, y, high], on_y(s)) for s in (1, 2, 3)]

    arrived(cols_s3)
    whole = cols_all[...].reshape(64, 128)
    cols_out[...] = jnp.where(z % 2 == 1, pltpu.roll(whole, 64, axis=1), whole)[:, :64]

    arrived(back_x0)
    back_c0 = send(core_all.at[c, :, :, low], core_all.at[c, :, :, low], mate())
    arrived(back_y1)
    back_c1 = send(core_all.at[c, :, :, high], core_all.at[c, :, :, high], mate())
    depth_s4.wait_recv()
    depth_out[...] = depth_all[...].reshape(64, 128)
    core_out[c] = core_all[c]
    back_c0.wait_recv()
    back_c1.wait_recv()
    core_out[o] = core_all[o]
    for copy in started:
        copy.wait_send()


def reduce_gradients(core, rows, cols, depth):
    vmem = pl.BlockSpec(memory_space=pltpu.VMEM)
    copies = 95

    def buf(*shape):
        return pltpu.VMEM(shape, f32)

    return pl.pallas_call(
        reduce_kernel,
        out_shape=(
            jax.ShapeDtypeStruct((2, 4, 4, 64, 128), f32),
            jax.ShapeDtypeStruct((16, 64), f32),
            jax.ShapeDtypeStruct((64, 64), f32),
            jax.ShapeDtypeStruct((64, 128), f32),
        ),
        in_specs=[vmem] * 4,
        out_specs=(vmem,) * 4,
        scratch_shapes=[
            buf(4, 4, 64, 128),
            buf(4, 4, 64, 128),
            buf(3, 4, 32, 128),
            buf(3, 4, 32, 128),
            buf(4, 32, 128),
            buf(4, 32, 128),
            buf(3, 32, 128),
            buf(3, 32, 128),
            buf(64, 128),
            buf(7, 8, 128),
            buf(64, 128),
            buf(2, 4, 4, 64, 128),
            buf(4, 64, 128),
            buf(4, 64, 128),
            buf(3, 64, 128),
            buf(128, 128),
            buf(7, 16, 128),
            buf(3, 4, 16, 128),
            buf(4, 16, 128),
            buf(7, 16, 128),
            buf(4, 16, 128),
            buf(4, 8, 128),
            buf(4, 8, 128),
            buf(3, 8, 128),
            buf(8, 128),
            buf(3, 8, 128),
            buf(2, 4, 8, 128),
            pltpu.SemaphoreType.DMA((copies,)),
            pltpu.SemaphoreType.DMA((copies,)),
        ],
        compiler_params=pltpu.CompilerParams(
            collective_id=1, has_side_effects=True, vmem_limit_bytes=33554432
        ),
        name="reduce_gradients",
    )(core, rows, cols, depth)


def unpack_kernel(core_ref, rows_ref, cols_ref, depth_ref, core_out, rows_out, cols_out, depth_out):
    core_out[0] = core_ref[:, :, :64]
    core_out[1] = core_ref[:, :, 64:]

    @pl.when(pl.program_id(0) == 0)
    def _():
        rows_out[...] = rows_ref[...]
        cols_out[...] = cols_ref[...]
        depth_out[...] = depth_ref[...]


def unpack_results(core, rows, cols, depth):
    steps = 4
    part = core.shape[0] // steps

    def whole(value):
        return pl.BlockSpec(value.shape, lambda step: (0, 0))

    return pl.pallas_call(
        unpack_kernel,
        out_shape=(
            jax.ShapeDtypeStruct((2, 32, 64, 64), f32),
            jax.ShapeDtypeStruct(rows.shape, f32),
            jax.ShapeDtypeStruct(cols.shape, f32),
            jax.ShapeDtypeStruct(depth.shape, f32),
        ),
        grid=(steps,),
        in_specs=[
            pl.BlockSpec((part, 64, 128), lambda step: (step, 0, 0)),
            whole(rows), whole(cols), whole(depth),
        ],
        out_specs=(
            pl.BlockSpec((2, part, 64, 64), lambda step: (0, step, 0, 0)),
            whole(rows), whole(cols), whole(depth),
        ),
        compiler_params=pltpu.CompilerParams(dimension_semantics=("arbitrary",), vmem_limit_bytes=8388608),
        name="unpack_results",
    )(core, rows, cols, depth)


def on_device(
    observed, weights, coords, counts, factor_rows, factor_cols, factor_depth, core_tensor
):
    rows, cols, slab, first = gather_factors(factor_rows.T, factor_cols, factor_depth, core_tensor)
    core_part, rows_part, cols_part, depth_part = block_gradients(
        coords, counts, observed.reshape(observed.shape[2:]), weights.reshape(weights.shape[2:]),
        first, rows, cols, slab, core_tensor,
    )
    core, rows_gradient, cols_gradient, depth_gradient = reduce_gradients(
        core_part.reshape(2, 4, 4, 64, 128),
        rows_part.reshape(4, 2, 64, 128),
        cols_part,
        depth_part.reshape(2, 4, 8, 128),
    )
    core, rows_gradient, cols_gradient, depth_gradient = unpack_results(
        core.reshape(32, 64, 128), rows_gradient, cols_gradient, depth_gradient
    )
    return (rows_gradient.T, cols_gradient, depth_gradient, core.reshape(64, 64, 64))


def solution(mesh):
    in_specs = (
        P("ia", "ja", "ka", None, None, None),
        P("ia", "ja", "ka", None, None, None),
        P("ia", "ja", "ka", None),
        P("ia", "ja", "ka"),
        P(None, ("ia", "ja", "ka")),
        P(None, ("ja", "ka")),
        P(),
        P(),
    )
    out_specs = (P(None, ("ia", "ja", "ka")), P(None, ("ja", "ka")), P(None, "ka"), P())
    return jax.shard_map(
        on_device, mesh=mesh, in_specs=in_specs, out_specs=out_specs, check_vma=False
    )
```

```python
import jax
import jax.numpy as jnp
from jax import lax
from jax.experimental import pallas as pl
from jax.experimental.pallas import tpu as pltpu
from jax.sharding import PartitionSpec as P

MESH = pl.DeviceIdType.MESH
f32 = jnp.float32
bf16 = jnp.bfloat16
resid_scale = 1.0 / 64.0

NN = (((1,), (0,)), ((), ()))
NT = (((1,), (1,)), ((), ()))
TN = (((0,), (0,)), ((), ()))


def dot(a, b, dims=NN):
    return lax.dot_general(a, b, dims, preferred_element_type=f32)


def low_lanes(shape):
    return lax.broadcasted_iota(jnp.int32, shape, len(shape) - 1) < 64


def unit(size):
    return (
        lax.broadcasted_iota(jnp.int32, (size, size), 0)
        == lax.broadcasted_iota(jnp.int32, (size, size), 1)
    ).astype(bf16)


def twice(value, axis):
    return jnp.concatenate([value, value], axis=axis)


def same(a, b):
    return (1 - jnp.minimum((a - b) * (a - b), 1)).astype(f32)


def split_terms(value):
    lead = value.astype(bf16)
    return lead, (value - lead.astype(f32)).astype(bf16)


def tucker_kernel(
    coords, counts, rows_hbm, cols_hbm, depth_hbm, core_hbm, data_hbm, weight_hbm,
    core_out, rows_out, cols_out, depth_out,
    rows_in, cols_in, slab_in, core_in, data_in, weight_in,
    row_buf, col_buf, slab_buf, first_wide, first_buf, mid, back_buf, core_own, rows_own_sum, cols_own_sum, depth_own,
    core_pair, core_sum, core_x, core_y, half_x, half_y, end_y, end_x, tile_sum, tile_in, tile_all, core_all,
    rows_pair, rows_sum, rows_x, rows_t, rows_z,
    cols_y, cols_sum, cols_z, cols_all,
    depth_pair, depth_sum, depth_x, depth_one, depth_y, depth_all,
    send_sem, recv_sem, local_sem, data_sem, weight_sem,
):
    y = lax.axis_index("ia")
    ja = lax.axis_index("ja")
    z = lax.axis_index("ka")
    x = ja // 2
    c = ja % 2
    o = 1 - c
    low = pl.ds(0, 32)
    high = pl.ds(32, 32)

    def fetch(src, dst, sem):
        copy = pltpu.make_async_copy(src, dst, sem)
        copy.start()
        return copy

    rows_copy = fetch(rows_hbm, rows_in, local_sem.at[0])
    cols_copy = fetch(cols_hbm, cols_in, local_sem.at[1])
    slab_copy = fetch(
        depth_hbm.at[:, pl.ds(pl.multiple_of(z * 128, 128), 128)], slab_in, local_sem.at[2]
    )
    core_copy = fetch(core_hbm, core_in, local_sem.at[3])

    def mate():
        return {"ja": x * 2 + o}

    def on_ja(step):
        return {"ja": (ja + step) % 8}

    def on_x(step):
        return {"ja": ((x + step) % 4) * 2 + c}

    def on_y(step):
        return {"ia": (y + step) % 4}

    def on_z(step):
        return {"ka": (z + step) % 8}

    barrier = pltpu.get_barrier_semaphore()
    targets = [on_z(s) for s in range(1, 8)] + [on_ja(s) for s in range(1, 8)] + [on_y(s) for s in (1, 2, 3)]
    for target in targets:
        pl.semaphore_signal(barrier, inc=1, device_id=target, device_id_type=MESH)

    slots = data_hbm.shape[0]
    for slot in range(slots):
        fetch(data_hbm.at[slot], data_in.at[slot], data_sem.at[slot])
        fetch(weight_hbm.at[slot], weight_in.at[slot], weight_sem.at[slot])

    started = []

    def send(src, dst, target):
        slot = len(started)
        copy = pltpu.make_async_remote_copy(
            src_ref=src, dst_ref=dst, send_sem=send_sem.at[slot], recv_sem=recv_sem.at[slot],
            device_id=target, device_id_type=MESH,
        )
        copy.start()
        started.append(copy)
        return copy

    def arrived(copies):
        for copy in copies:
            copy.wait_recv()

    rows_copy.wait()
    own_rows = dot(rows_in[...], twice(unit(64), 1))
    row_buf[ja, z] = jnp.where(low_lanes((8, 128)), own_rows[:8], own_rows[8:]).astype(bf16)
    cols_copy.wait()
    own_cols = dot(unit(64), twice(cols_in[...], 0), NT)
    col_buf[z] = jnp.where(low_lanes((32, 128)), own_cols[:32], own_cols[32:]).astype(bf16)
    pl.semaphore_wait(barrier, len(targets))
    order = (4, 3, 5, 2, 6, 1, 7)
    deep_rows = [send(row_buf.at[ja, z], row_buf.at[ja, z], on_z(s)) for s in order]
    deep_cols = [send(col_buf.at[z], col_buf.at[z], on_z(s)) for s in order]

    slab_copy.wait()
    slab_turned = dot(unit(128), slab_in[...], NT)
    slab_buf[...] = slab_turned.reshape(8, 16, 64)
    slab_rows = jnp.concatenate(
        [slab_turned[t * 32 + half * 16 : t * 32 + half * 16 + 16] for half in range(2) for t in range(4)], axis=0
    ).astype(bf16)
    core_copy.wait()

    def first_of(pair, carry):
        left = core_in[pair * 2]
        right = core_in[pair * 2 + 1]
        both = dot(slab_rows, jnp.concatenate([left, left, right, right], axis=0), NT)
        for side in range(2):
            piece = both[:, side * 128 : side * 128 + 128]
            first_wide[pl.ds(pair * 2 + side, 64, stride=65), :] = jnp.where(
                low_lanes((64, 128)), piece[:64], piece[64:]
            )
        return carry

    lax.fori_loop(0, 32, first_of, 0, unroll=4)

    arrived(deep_rows)
    wide_rows = [send(row_buf.at[ja], row_buf.at[ja], on_ja(s)) for s in order]

    def round_of(step, carry):
        first_buf[step] = first_wide[pl.ds(step * 65, 64), :].astype(bf16)
        return carry

    lax.fori_loop(0, 64, round_of, 0, unroll=8)
    rows_own_sum[...] = jnp.zeros_like(rows_own_sum)
    cols_own_sum[...] = jnp.zeros_like(cols_own_sum)
    arrived(deep_cols)
    arrived(wide_rows)

    live_count = counts[0, 0, 0]

    def place(slot):
        p = coords[0, 0, 0, slot] & 7
        q = coords[0, 1, 0, slot] & 3
        t = coords[0, 2, 0, slot] & 3
        return p, q, t

    def one_slot(slot, carry):
        p, q, t = place(slot)
        alive = jnp.clip(live_count - slot, 0, 1).astype(f32)
        packed_rows = row_buf[p].astype(f32).reshape(64, 128)
        turned_rows = pltpu.roll(packed_rows, 64, axis=1)
        row_t = jnp.concatenate(
            [part[s * 8 : s * 8 + 8] for s in range(8) for part in (packed_rows, turned_rows)], axis=0
        )[:, :64].astype(bf16)
        row_n = (dot(unit(64), row_t, NT) * alive).astype(bf16)
        row_n2 = twice(row_n, 1)
        packed_cols = jnp.concatenate([col_buf[q * 2], col_buf[q * 2 + 1]], axis=0).astype(f32)
        turned_cols = pltpu.roll(packed_cols, 64, axis=1)
        left = low_lanes((64, 128))
        first_half = jnp.where(left, packed_cols, turned_cols)
        second_half = jnp.where(left, turned_cols, packed_cols)
        col_t = jnp.concatenate(
            [first_half[:32], second_half[:32], first_half[32:], second_half[32:]], axis=0
        )
        left = low_lanes((128, 128))
        zero = jnp.zeros((128, 128), f32)
        col_low = jnp.where(left, col_t, zero)
        col_high = jnp.where(left, zero, col_t)
        to_model = jnp.concatenate([twice(col_low, 1), twice(col_high, 1)], axis=0).astype(bf16)
        to_back = (jnp.concatenate([col_low, col_high], axis=0) * resid_scale).astype(bf16)

        def forward(pair, carry):
            kk = pair * 2
            part = dot(
                row_t, jnp.concatenate([first_buf[t * 16 + kk], first_buf[t * 16 + kk + 1]], axis=1)
            )
            mid[pl.ds(kk, 128, stride=17), :] = part[:, :128]
            mid[pl.ds(kk + 1, 128, stride=17), :] = part[:, 128:]
            return carry

        lax.fori_loop(0, 8, forward, 0, unroll=8)
        pltpu.make_async_copy(data_hbm.at[slot], data_in.at[slot], data_sem.at[slot]).wait()
        pltpu.make_async_copy(weight_hbm.at[slot], weight_in.at[slot], weight_sem.at[slot]).wait()

        def middle(step, col_part):
            base = step * 16
            lead, rest = split_terms(
                jnp.concatenate([mid[pl.ds((base + i) * 17, 16), :] for i in range(16)], axis=0)
            )
            model = dot(jnp.concatenate([lead, rest], axis=1), to_model, NT)

            def half_of(half):
                at = (slot, pl.ds(base, 16), pl.ds(half * 16, 16), slice(None))
                data = data_in[at].reshape(256, 128).astype(f32)
                weight = weight_in[at].reshape(256, 128).astype(f32)
                return (weight * (model[:, half * 128 : half * 128 + 128] - data)).astype(bf16)

            residual = jnp.concatenate([half_of(0), half_of(1)], axis=1)
            back = dot(residual, to_back)
            for i in range(16):
                mid[pl.ds((base + i) * 17, 16), :] = back[i * 16 : i * 16 + 16]
            return col_part + dot(lead, residual, TN)

        col_part = lax.fori_loop(0, 8, middle, jnp.zeros((128, 256), f32), unroll=MIDDLE)
        col_part = (col_part[:64, :128] + col_part[64:, 128:]) * resid_scale
        for part in range(4):
            cols_own_sum[part] += col_part * (same(q, part) * alive)

        def backward(kk, row_part):
            lead, rest = split_terms(mid[pl.ds(kk, 128, stride=17), :])
            both = dot(row_n2, jnp.concatenate([lead, rest], axis=0))
            back_buf[pl.ds((slot * 16 + kk) * 65, 64), :] = both.astype(bf16).astype(f32)
            return row_part + dot(
                twice(first_buf[t * 16 + kk], 1), jnp.concatenate([lead, rest], axis=1), NT
            )

        row_part = lax.fori_loop(0, 16, backward, jnp.zeros((64, 128), f32), unroll=16)
        for part in range(8):
            rows_own_sum[part // 2, part % 2] += row_part * (same(p, part) * alive)
        return carry

    lax.fori_loop(0, slots, one_slot, 0)

    rows_c = send(rows_own_sum.at[:, o], rows_pair, mate())
    cols_s1 = [
        send(cols_own_sum.at[:, pl.ds(pl.multiple_of(((y + s) % 4) * 16, 16), 16), :], cols_y.at[s - 1], on_y(s))
        for s in (1, 2, 3)
    ]

    slab_slots = jnp.concatenate(
        [
            slab_buf[place(slot)[2] * 2 + half]
            for half in range(2)
            for slot in range(slots)
        ],
        axis=0,
    ).astype(bf16)
    slab_n = dot(unit(64), slab_slots, NT).astype(bf16)
    tall = slots * 16
    left_tall = low_lanes((tall, 128))

    def finish_group(half, group, depth_part):
        def finish(step, depth_part):
            u = half * 16 + group * 4 + step
            one = back_buf[pl.ds(u, tall, stride=65), :]
            two = back_buf[pl.ds(u + 32, tall, stride=65), :]
            both = jnp.concatenate(
                [
                    jnp.where(left_tall, one, pltpu.roll(two, 64, axis=1)),
                    jnp.where(left_tall, pltpu.roll(one, 64, axis=1), two),
                ],
                axis=0,
            ).astype(bf16)
            core_own[half, group, step] = dot(slab_n, both)
            piece = jnp.concatenate([core_in[u], core_in[u + 32]], axis=0)
            return depth_part + dot(both, piece)

        return lax.fori_loop(0, 4, finish, depth_part, unroll=4)

    depth_part = jnp.zeros((2 * tall, 64), f32)
    core_c = []
    for group in range(4):
        depth_part = finish_group(o, group, depth_part)
        core_c.append(send(core_own.at[o, group], core_pair.at[group], mate()))
    rows_c.wait_recv()
    rows_sum[...] = rows_own_sum[:, c] + rows_pair[...]
    rows_s1 = [send(rows_sum.at[(x + s) % 4], rows_x.at[s - 1], on_x(s)) for s in (1, 2, 3)]
    for group in range(4):
        depth_part = finish_group(c, group, depth_part)

    depth_pieces = []
    for t in range(4):
        for half in range(2):
            piece = jnp.zeros((16, 64), f32)
            for slot in range(slots):
                at = half * tall + slot * 16
                piece = piece + depth_part[at : at + 16] * same(place(slot)[2], t)
            depth_pieces.append(piece)
    depth_turned = jnp.concatenate(
        [jnp.concatenate(depth_pieces, axis=0), jnp.zeros((128, 64), f32)], axis=1
    ).T[:64]
    depth_own[...] = depth_turned.reshape(2, 4, 8, 128)
    depth_c = send(depth_own.at[o], depth_pair, mate())

    core_x0 = []
    for group in range(4):
        core_c[group].wait_recv()
        core_sum[group] = core_own[c, group] + core_pair[group]
    core_x0 = [send(core_sum.at[(x + s) % 4, :, low], core_x.at[s - 1], on_x(s)) for s in (2, 1, 3)]
    core_y1 = [send(core_sum.at[:, (y + s) % 4, high], core_y.at[s - 1], on_y(s)) for s in (2, 1, 3)]
    depth_c.wait_recv()
    depth_sum[...] = depth_own[c] + depth_pair[...]
    depth_s1 = [send(depth_sum.at[(x + s) % 4], depth_x.at[s - 1], on_x(s)) for s in (1, 2, 3)]

    arrived(cols_s1)
    cols_sum[...] = (
        cols_own_sum[:, pl.ds(pl.multiple_of(y * 16, 16), 16), :] + cols_y[0] + cols_y[1] + cols_y[2]
    )
    cols_s2 = [send(cols_sum.at[((z + s) % 8) // 2], cols_z.at[s - 1], on_z(s)) for s in range(1, 8)]

    arrived(core_x0)
    half_x[...] = core_sum[x, :, low] + core_x[0] + core_x[1] + core_x[2]
    core_y0 = [send(half_x.at[(y + s) % 4], end_y.at[s - 1], on_y(s)) for s in (1, 2, 3)]
    arrived(core_y1)
    half_y[...] = core_sum[:, y, high] + core_y[0] + core_y[1] + core_y[2]
    core_x1 = [send(half_y.at[(x + s) % 4], end_x.at[s - 1], on_x(s)) for s in (1, 2, 3)]

    arrived(rows_s1)
    rows_own = rows_sum[x] + rows_x[0] + rows_x[1] + rows_x[2]
    rows_t[...] = jnp.concatenate([rows_own, jnp.zeros((64, 128), f32)], axis=0).T
    rows_s2 = [
        send(rows_t.at[pl.ds(pl.multiple_of(((z + s) % 8) * 16, 16), 16), :], rows_z.at[s - 1], on_z(s))
        for s in range(1, 8)
    ]
    arrived(depth_s1)
    depth_one[...] = depth_sum[x] + depth_x[0] + depth_x[1] + depth_x[2]
    depth_s2 = [send(depth_one, depth_y.at[s - 1], on_y(s)) for s in (1, 2, 3)]

    arrived(core_y0)
    tile_sum[low] = half_x[y] + end_y[0] + end_y[1] + end_y[2]
    arrived(core_x1)
    tile_sum[high] = half_y[x] + end_x[0] + end_x[1] + end_x[2]
    core_z = [
        send(tile_sum.at[pl.ds(pl.multiple_of(((z + s) % 8) * 8, 8), 8), :], tile_in.at[s - 1], on_z(s))
        for s in range(1, 8)
    ]

    arrived(cols_s2)
    col_total = cols_sum[z // 2]
    for s in range(7):
        col_total = col_total + cols_z[s]
    cols_all[y] = col_total
    cols_s3 = [send(cols_all.at[y], cols_all.at[y], on_y(s)) for s in (1, 2, 3)]
    arrived(depth_s2)
    depth_all[c, x] = depth_one[...] + depth_y[0] + depth_y[1] + depth_y[2]
    depth_s3 = [send(depth_all.at[c, x], depth_all.at[c, x], on_x(s)) for s in (1, 2, 3)]
    arrived(rows_s2)
    row_total = rows_t[pl.ds(pl.multiple_of(z * 16, 16), 16), :]
    for s in range(7):
        row_total = row_total + rows_z[s]
    rows_out[...] = row_total[:, :64]

    own = pl.ds(pl.multiple_of(z * 8, 8), 8)
    arrived(core_z)
    total = tile_sum[own, :]
    for s in range(7):
        total = total + tile_in[s]
    tile_all[own, :] = total
    core_g = [send(tile_all.at[own, :], tile_all.at[own, :], on_z(s)) for s in range(1, 8)]
    arrived(depth_s3)
    depth_s4 = send(depth_all.at[c], depth_all.at[c], mate())
    arrived(core_g)
    turned = jnp.concatenate([tile_all[...], jnp.zeros((64, 128), f32)], axis=0).T
    core_all[c, x, y] = turned[:64] + pltpu.roll(turned[64:], 64, axis=1)

    back_y0 = [send(core_all.at[c, x, y, low], core_all.at[c, x, y, low], on_y(s)) for s in (1, 2, 3)]
    back_x1 = [send(core_all.at[c, x, y, high], core_all.at[c, x, y, high], on_x(s)) for s in (1, 2, 3)]
    arrived(back_y0)
    back_x0 = [send(core_all.at[c, x, :, low], core_all.at[c, x, :, low], on_x(s)) for s in (1, 2, 3)]
    arrived(back_x1)
    back_y1 = [send(core_all.at[c, :, y, high], core_all.at[c, :, y, high], on_y(s)) for s in (1, 2, 3)]

    arrived(cols_s3)
    whole = cols_all[...].reshape(64, 128)
    cols_out[...] = jnp.where(z % 2 == 1, pltpu.roll(whole, 64, axis=1), whole)[:, :64]

    arrived(back_x0)
    back_c0 = send(core_all.at[c, :, :, low], core_all.at[c, :, :, low], mate())
    arrived(back_y1)
    back_c1 = send(core_all.at[c, :, :, high], core_all.at[c, :, :, high], mate())
    depth_s4.wait_recv()
    depth_out[...] = depth_all[...].reshape(64, 128)
    own_half = fetch(core_all.at[c], core_out.at[c], local_sem.at[4])
    back_c0.wait_recv()
    back_c1.wait_recv()
    other_half = fetch(core_all.at[o], core_out.at[o], local_sem.at[5])
    for copy in started:
        copy.wait_send()
    own_half.wait()
    other_half.wait()


MIDDLE = 4


def tucker_gradients(coords, counts, rows, cols, depth, core, data, weights):
    vmem = pl.BlockSpec(memory_space=pltpu.VMEM)
    smem = pl.BlockSpec(memory_space=pltpu.SMEM)
    hbm = pl.BlockSpec(memory_space=pltpu.HBM)
    slots = data.shape[0]
    copies = 110

    def buf(*shape):
        return pltpu.VMEM(shape, f32)

    def buf16(*shape):
        return pltpu.VMEM(shape, bf16)

    return pl.pallas_call(
        tucker_kernel,
        out_shape=(
            jax.ShapeDtypeStruct((2, 4, 4, 64, 128), f32),
            jax.ShapeDtypeStruct((16, 64), f32),
            jax.ShapeDtypeStruct((64, 64), f32),
            jax.ShapeDtypeStruct((64, 128), f32),
        ),
        in_specs=[smem, smem] + [hbm] * 6,
        out_specs=(hbm, vmem, vmem, vmem),
        scratch_shapes=[
            buf16(16, 64),
            buf16(64, 64),
            buf16(64, 128),
            buf16(64, 64, 64),
            buf16(slots, 128, 32, 128),
            buf16(slots, 128, 32, 128),
            buf16(8, 8, 8, 128),
            buf16(8, 32, 128),
            buf(8, 16, 64),
            buf(64 * 65, 128),
            buf16(64, 64, 128),
            buf(128 * 17, 128),
            buf(slots * 16 * 65, 128),
            buf(2, 4, 4, 64, 128),
            buf(4, 2, 64, 128),
            buf(4, 64, 128),
            buf(2, 4, 8, 128),
            buf(4, 4, 64, 128),
            buf(4, 4, 64, 128),
            buf(3, 4, 32, 128),
            buf(3, 4, 32, 128),
            buf(4, 32, 128),
            buf(4, 32, 128),
            buf(3, 32, 128),
            buf(3, 32, 128),
            buf(64, 128),
            buf(7, 8, 128),
            buf(64, 128),
            buf(2, 4, 4, 64, 128),
            buf(4, 64, 128),
            buf(4, 64, 128),
            buf(3, 64, 128),
            buf(128, 128),
            buf(7, 16, 128),
            buf(3, 4, 16, 128),
            buf(4, 16, 128),
            buf(7, 16, 128),
            buf(4, 16, 128),
            buf(4, 8, 128),
            buf(4, 8, 128),
            buf(3, 8, 128),
            buf(8, 128),
            buf(3, 8, 128),
            buf(2, 4, 8, 128),
            pltpu.SemaphoreType.DMA((copies,)),
            pltpu.SemaphoreType.DMA((copies,)),
            pltpu.SemaphoreType.DMA((6,)),
            pltpu.SemaphoreType.DMA((slots,)),
            pltpu.SemaphoreType.DMA((slots,)),
        ],
        compiler_params=pltpu.CompilerParams(
            collective_id=0, has_side_effects=True, vmem_limit_bytes=67043328
        ),
        name="tucker_gradients",
    )(coords, counts, rows, cols, depth, core, data, weights)


def unpack_kernel(core_ref, rows_ref, cols_ref, depth_ref, core_out, rows_out, cols_out, depth_out):
    core_out[0] = core_ref[:, :, :64]
    core_out[1] = core_ref[:, :, 64:]

    @pl.when(pl.program_id(0) == 0)
    def _():
        rows_out[...] = rows_ref[...]
        cols_out[...] = cols_ref[...]
        depth_out[...] = depth_ref[...]


def unpack_results(core, rows, cols, depth):
    steps = 4
    part = core.shape[0] // steps

    def whole(value):
        return pl.BlockSpec(value.shape, lambda step: (0, 0))

    return pl.pallas_call(
        unpack_kernel,
        out_shape=(
            jax.ShapeDtypeStruct((2, 32, 64, 64), f32),
            jax.ShapeDtypeStruct(rows.shape, f32),
            jax.ShapeDtypeStruct(cols.shape, f32),
            jax.ShapeDtypeStruct(depth.shape, f32),
        ),
        grid=(steps,),
        in_specs=[
            pl.BlockSpec((part, 64, 128), lambda step: (step, 0, 0)),
            whole(rows), whole(cols), whole(depth),
        ],
        out_specs=(
            pl.BlockSpec((2, part, 64, 64), lambda step: (0, step, 0, 0)),
            whole(rows), whole(cols), whole(depth),
        ),
        compiler_params=pltpu.CompilerParams(dimension_semantics=("arbitrary",), vmem_limit_bytes=67043328),
        name="unpack_results",
    )(core, rows, cols, depth)


def on_device(
    observed, weights, coords, counts, factor_rows, factor_cols, factor_depth, core_tensor
):
    core, rows_gradient, cols_gradient, depth_gradient = tucker_gradients(
        coords.transpose(0, 3, 1, 2), counts, factor_rows.T, factor_cols, factor_depth, core_tensor,
        observed.reshape(observed.shape[2:]), weights.reshape(weights.shape[2:]),
    )
    core, rows_gradient, cols_gradient, depth_gradient = unpack_results(
        core.reshape(32, 64, 128), rows_gradient, cols_gradient, depth_gradient
    )
    return (rows_gradient.T, cols_gradient, depth_gradient, core.reshape(64, 64, 64))


def solution(mesh):
    in_specs = (
        P("ia", "ja", "ka", None, None, None),
        P("ia", "ja", "ka", None, None, None),
        P("ia", "ja", "ka", None),
        P("ia", "ja", "ka"),
        P(None, ("ia", "ja", "ka")),
        P(None, ("ja", "ka")),
        P(),
        P(),
    )
    out_specs = (P(None, ("ia", "ja", "ka")), P(None, ("ja", "ka")), P(None, "ka"), P())
    return jax.shard_map(
        on_device, mesh=mesh, in_specs=in_specs, out_specs=out_specs, check_vma=False
    )
```

```python
import jax
import jax.numpy as jnp
from jax import lax
from jax.experimental import pallas as pl
from jax.experimental.pallas import tpu as pltpu
from jax.sharding import PartitionSpec as P

MESH = pl.DeviceIdType.MESH
f32 = jnp.float32
bf16 = jnp.bfloat16
resid_scale = 1.0 / 64.0

NN = (((1,), (0,)), ((), ()))
NT = (((1,), (1,)), ((), ()))
TN = (((0,), (0,)), ((), ()))


def dot(a, b, dims=NN):
    return lax.dot_general(a, b, dims, preferred_element_type=f32)


def low_lanes(shape):
    return lax.broadcasted_iota(jnp.int32, shape, len(shape) - 1) < 64


def unit(size):
    return (
        lax.broadcasted_iota(jnp.int32, (size, size), 0)
        == lax.broadcasted_iota(jnp.int32, (size, size), 1)
    ).astype(bf16)


def twice(value, axis):
    return jnp.concatenate([value, value], axis=axis)


def same(a, b):
    return (1 - jnp.minimum((a - b) * (a - b), 1)).astype(f32)


def split_terms(value):
    lead = value.astype(bf16)
    return lead, (value - lead.astype(f32)).astype(bf16)


def tucker_kernel(
    coords, counts, rows_hbm, cols_hbm, depth_hbm, core_hbm, data_hbm, weight_hbm,
    core_out, rows_out, cols_out, depth_out,
    rows_in, cols_in, slab_in, core_in, data_in, weight_in,
    row_buf, col_buf, slab_buf, first_wide, first_buf, mid, back_buf, core_own, rows_own_sum, cols_own_sum, depth_own,
    core_pair, core_sum, core_x, core_y, half_x, half_y, end_y, end_x, tile_sum, tile_in, tile_all, core_all,
    rows_pair, rows_sum, rows_x, rows_t, rows_z,
    cols_y, cols_sum, cols_z, cols_all,
    depth_pair, depth_sum, depth_x, depth_one, depth_y, depth_all,
    send_sem, recv_sem, local_sem, data_sem, weight_sem,
):
    y = lax.axis_index("ia")
    ja = lax.axis_index("ja")
    z = lax.axis_index("ka")
    x = ja // 2
    c = ja % 2
    o = 1 - c
    low = pl.ds(0, 32)
    high = pl.ds(32, 32)

    def fetch(src, dst, sem):
        copy = pltpu.make_async_copy(src, dst, sem)
        copy.start()
        return copy

    rows_copy = fetch(rows_hbm, rows_in, local_sem.at[0])
    cols_copy = fetch(cols_hbm, cols_in, local_sem.at[1])
    slab_copy = fetch(
        depth_hbm.at[:, pl.ds(pl.multiple_of(z * 128, 128), 128)], slab_in, local_sem.at[2]
    )
    core_copy = fetch(core_hbm, core_in, local_sem.at[3])

    def mate():
        return {"ja": x * 2 + o}

    def on_ja(step):
        return {"ja": (ja + step) % 8}

    def on_x(step):
        return {"ja": ((x + step) % 4) * 2 + c}

    def on_y(step):
        return {"ia": (y + step) % 4}

    def on_z(step):
        return {"ka": (z + step) % 8}

    barrier = pltpu.get_barrier_semaphore()
    targets = [on_z(s) for s in range(1, 8)] + [on_ja(s) for s in range(1, 8)] + [on_y(s) for s in (1, 2, 3)]
    for target in targets:
        pl.semaphore_signal(barrier, inc=1, device_id=target, device_id_type=MESH)

    slots = data_hbm.shape[0]
    for slot in range(slots):
        fetch(data_hbm.at[slot], data_in.at[slot], data_sem.at[slot])
        fetch(weight_hbm.at[slot], weight_in.at[slot], weight_sem.at[slot])

    started = []

    def send(src, dst, target):
        slot = len(started)
        copy = pltpu.make_async_remote_copy(
            src_ref=src, dst_ref=dst, send_sem=send_sem.at[slot], recv_sem=recv_sem.at[slot],
            device_id=target, device_id_type=MESH,
        )
        copy.start()
        started.append(copy)
        return copy

    def arrived(copies):
        for copy in copies:
            copy.wait_recv()

    rows_copy.wait()
    own_rows = dot(rows_in[...], twice(unit(64), 1))
    row_buf[ja, z] = jnp.where(low_lanes((8, 128)), own_rows[:8], own_rows[8:]).astype(bf16)
    cols_copy.wait()
    own_cols = dot(unit(64), twice(cols_in[...], 0), NT)
    col_buf[z] = jnp.where(low_lanes((32, 128)), own_cols[:32], own_cols[32:]).astype(bf16)
    pl.semaphore_wait(barrier, len(targets))
    order = (4, 3, 5, 2, 6, 1, 7)
    deep_rows = [send(row_buf.at[ja, z], row_buf.at[ja, z], on_z(s)) for s in order]
    deep_cols = [send(col_buf.at[z], col_buf.at[z], on_z(s)) for s in order]

    slab_copy.wait()
    slab_turned = dot(unit(128), slab_in[...], NT)
    slab_buf[...] = slab_turned.reshape(8, 16, 64)
    slab_rows = jnp.concatenate(
        [slab_turned[t * 32 + half * 16 : t * 32 + half * 16 + 16] for half in range(2) for t in range(4)], axis=0
    ).astype(bf16)
    core_copy.wait()

    def first_of(pair, carry):
        left = core_in[pair * 2]
        right = core_in[pair * 2 + 1]
        both = dot(slab_rows, jnp.concatenate([left, left, right, right], axis=0), NT)
        for side in range(2):
            piece = both[:, side * 128 : side * 128 + 128]
            first_wide[pl.ds(pair * 2 + side, 64, stride=65), :] = jnp.where(
                low_lanes((64, 128)), piece[:64], piece[64:]
            )
        return carry

    lax.fori_loop(0, 32, first_of, 0, unroll=4)

    arrived(deep_rows)
    wide_rows = [send(row_buf.at[ja], row_buf.at[ja], on_ja(s)) for s in order]

    def round_of(step, carry):
        first_buf[step] = first_wide[pl.ds(step * 65, 64), :].astype(bf16)
        return carry

    lax.fori_loop(0, 64, round_of, 0, unroll=8)
    rows_own_sum[...] = jnp.zeros_like(rows_own_sum)
    cols_own_sum[...] = jnp.zeros_like(cols_own_sum)
    arrived(deep_cols)
    arrived(wide_rows)

    live_count = counts[0, 0, 0]

    def place(slot):
        p = coords[0, 0, 0, slot] & 7
        q = coords[0, 1, 0, slot] & 3
        t = coords[0, 2, 0, slot] & 3
        return p, q, t

    def one_slot(slot, carry):
        p, q, t = place(slot)
        alive = jnp.clip(live_count - slot, 0, 1).astype(f32)
        packed_rows = row_buf[p].astype(f32).reshape(64, 128)
        turned_rows = pltpu.roll(packed_rows, 64, axis=1)
        row_t = jnp.concatenate(
            [part[s * 8 : s * 8 + 8] for s in range(8) for part in (packed_rows, turned_rows)], axis=0
        )[:, :64].astype(bf16)
        row_n = (dot(unit(64), row_t, NT) * alive).astype(bf16)
        row_n2 = twice(row_n, 1)
        packed_cols = jnp.concatenate([col_buf[q * 2], col_buf[q * 2 + 1]], axis=0).astype(f32)
        turned_cols = pltpu.roll(packed_cols, 64, axis=1)
        left = low_lanes((64, 128))
        first_half = jnp.where(left, packed_cols, turned_cols)
        second_half = jnp.where(left, turned_cols, packed_cols)
        col_t = jnp.concatenate(
            [first_half[:32], second_half[:32], first_half[32:], second_half[32:]], axis=0
        )
        left = low_lanes((128, 128))
        zero = jnp.zeros((128, 128), f32)
        col_low = jnp.where(left, col_t, zero)
        col_high = jnp.where(left, zero, col_t)
        to_model = jnp.concatenate([twice(col_low, 1), twice(col_high, 1)], axis=0).astype(bf16)
        to_back = (jnp.concatenate([col_low, col_high], axis=0) * resid_scale).astype(bf16)

        def forward(pair, carry):
            kk = pair * 2
            part = dot(
                row_t, jnp.concatenate([first_buf[t * 16 + kk], first_buf[t * 16 + kk + 1]], axis=1)
            )
            mid[pl.ds(kk, 128, stride=17), :] = part[:, :128]
            mid[pl.ds(kk + 1, 128, stride=17), :] = part[:, 128:]
            return carry

        lax.fori_loop(0, 8, forward, 0, unroll=8)
        pltpu.make_async_copy(data_hbm.at[slot], data_in.at[slot], data_sem.at[slot]).wait()
        pltpu.make_async_copy(weight_hbm.at[slot], weight_in.at[slot], weight_sem.at[slot]).wait()

        def middle(step, col_part):
            base = step * 16
            lead, rest = split_terms(
                jnp.concatenate([mid[pl.ds((base + i) * 17, 16), :] for i in range(16)], axis=0)
            )
            model = dot(jnp.concatenate([lead, rest], axis=1), to_model, NT)

            def half_of(half):
                at = (slot, pl.ds(base, 16), pl.ds(half * 16, 16), slice(None))
                data = data_in[at].reshape(256, 128).astype(f32)
                weight = weight_in[at].reshape(256, 128).astype(f32)
                return (weight * (model[:, half * 128 : half * 128 + 128] - data)).astype(bf16)

            residual = jnp.concatenate([half_of(0), half_of(1)], axis=1)
            back = dot(residual, to_back)
            for i in range(16):
                mid[pl.ds((base + i) * 17, 16), :] = back[i * 16 : i * 16 + 16]
            return col_part + dot(lead, residual, TN)

        col_part = lax.fori_loop(0, 8, middle, jnp.zeros((128, 256), f32), unroll=MIDDLE)
        col_part = (col_part[:64, :128] + col_part[64:, 128:]) * resid_scale
        for part in range(4):
            cols_own_sum[part] += col_part * (same(q, part) * alive)

        def backward(kk, row_part):
            lead, rest = split_terms(mid[pl.ds(kk, 128, stride=17), :])
            both = dot(row_n2, jnp.concatenate([lead, rest], axis=0))
            back_buf[pl.ds((slot * 16 + kk) * 65, 64), :] = both.astype(bf16).astype(f32)
            return row_part + dot(
                twice(first_buf[t * 16 + kk], 1), jnp.concatenate([lead, rest], axis=1), NT
            )

        row_part = lax.fori_loop(0, 16, backward, jnp.zeros((64, 128), f32), unroll=16)
        for part in range(8):
            rows_own_sum[part // 2, part % 2] += row_part * (same(p, part) * alive)
        return carry

    lax.fori_loop(0, slots, one_slot, 0)

    rows_c = send(rows_own_sum.at[:, o], rows_pair, mate())
    cols_s1 = [
        send(cols_own_sum.at[:, pl.ds(pl.multiple_of(((y + s) % 4) * 16, 16), 16), :], cols_y.at[s - 1], on_y(s))
        for s in (1, 2, 3)
    ]

    slab_slots = jnp.concatenate(
        [
            slab_buf[place(slot)[2] * 2 + half]
            for half in range(2)
            for slot in range(slots)
        ],
        axis=0,
    ).astype(bf16)
    slab_n = dot(unit(64), slab_slots, NT).astype(bf16)
    tall = slots * 16
    left_tall = low_lanes((tall, 128))

    def finish_group(half, group, depth_part):
        def finish(step, depth_part):
            u = half * 16 + group * 4 + step
            one = back_buf[pl.ds(u, tall, stride=65), :]
            two = back_buf[pl.ds(u + 32, tall, stride=65), :]
            both = jnp.concatenate(
                [
                    jnp.where(left_tall, one, pltpu.roll(two, 64, axis=1)),
                    jnp.where(left_tall, pltpu.roll(one, 64, axis=1), two),
                ],
                axis=0,
            ).astype(bf16)
            core_own[half, group, step] = dot(slab_n, both)
            piece = jnp.concatenate([core_in[u], core_in[u + 32]], axis=0)
            return depth_part + dot(both, piece)

        return lax.fori_loop(0, 4, finish, depth_part, unroll=4)

    depth_part = jnp.zeros((2 * tall, 64), f32)
    core_c = []
    for group in range(4):
        depth_part = finish_group(o, group, depth_part)
        core_c.append(send(core_own.at[o, group], core_pair.at[group], mate()))
    rows_c.wait_recv()
    rows_sum[...] = rows_own_sum[:, c] + rows_pair[...]
    rows_s1 = [send(rows_sum.at[(x + s) % 4], rows_x.at[s - 1], on_x(s)) for s in (1, 2, 3)]
    for group in range(4):
        depth_part = finish_group(c, group, depth_part)

    depth_pieces = []
    for t in range(4):
        for half in range(2):
            piece = jnp.zeros((16, 64), f32)
            for slot in range(slots):
                at = half * tall + slot * 16
                piece = piece + depth_part[at : at + 16] * same(place(slot)[2], t)
            depth_pieces.append(piece)
    depth_turned = jnp.concatenate(
        [jnp.concatenate(depth_pieces, axis=0), jnp.zeros((128, 64), f32)], axis=1
    ).T[:64]
    depth_own[...] = depth_turned.reshape(2, 4, 8, 128)
    depth_c = send(depth_own.at[o], depth_pair, mate())

    for group in range(4):
        core_c[group].wait_recv()
        core_sum[group] = core_own[c, group] + core_pair[group]
    far_first = (2, 1, 3)
    core_x0, core_y1 = {}, {}
    for other in (2, 1, 3, 0):
        at_y = (y + other) % 4
        at_x = (x + other) % 4
        core_x0[other] = [
            send(core_sum.at[(x + s) % 4, at_y, low], core_x.at[s - 1, at_y], on_x(s)) for s in far_first
        ]
        core_y1[other] = [
            send(core_sum.at[at_x, (y + s) % 4, high], core_y.at[s - 1, at_x], on_y(s)) for s in far_first
        ]
    depth_c.wait_recv()
    depth_sum[...] = depth_own[c] + depth_pair[...]
    depth_s1 = [send(depth_sum.at[(x + s) % 4], depth_x.at[s - 1], on_x(s)) for s in (1, 2, 3)]

    arrived(cols_s1)
    cols_sum[...] = (
        cols_own_sum[:, pl.ds(pl.multiple_of(y * 16, 16), 16), :] + cols_y[0] + cols_y[1] + cols_y[2]
    )
    cols_s2 = [send(cols_sum.at[((z + s) % 8) // 2], cols_z.at[s - 1], on_z(s)) for s in range(1, 8)]

    core_y0, core_x1 = [], []
    for other in (2, 1, 3, 0):
        at_y = (y + other) % 4
        at_x = (x + other) % 4
        arrived(core_x0[other])
        half_x[at_y] = core_sum[x, at_y, low] + core_x[0, at_y] + core_x[1, at_y] + core_x[2, at_y]
        if other:
            core_y0.append(send(half_x.at[at_y], end_y.at[other - 1], on_y(other)))
        arrived(core_y1[other])
        half_y[at_x] = core_sum[at_x, y, high] + core_y[0, at_x] + core_y[1, at_x] + core_y[2, at_x]
        if other:
            core_x1.append(send(half_y.at[at_x], end_x.at[other - 1], on_x(other)))

    arrived(rows_s1)
    rows_own = rows_sum[x] + rows_x[0] + rows_x[1] + rows_x[2]
    rows_t[...] = jnp.concatenate([rows_own, jnp.zeros((64, 128), f32)], axis=0).T
    rows_s2 = [
        send(rows_t.at[pl.ds(pl.multiple_of(((z + s) % 8) * 16, 16), 16), :], rows_z.at[s - 1], on_z(s))
        for s in range(1, 8)
    ]
    arrived(depth_s1)
    depth_one[...] = depth_sum[x] + depth_x[0] + depth_x[1] + depth_x[2]
    depth_s2 = [send(depth_one, depth_y.at[s - 1], on_y(s)) for s in (1, 2, 3)]

    arrived(core_y0)
    tile_sum[low] = half_x[y] + end_y[0] + end_y[1] + end_y[2]
    arrived(core_x1)
    tile_sum[high] = half_y[x] + end_x[0] + end_x[1] + end_x[2]
    core_z = [
        send(tile_sum.at[pl.ds(pl.multiple_of(((z + s) % 8) * 8, 8), 8), :], tile_in.at[s - 1], on_z(s))
        for s in range(1, 8)
    ]

    arrived(cols_s2)
    col_total = cols_sum[z // 2]
    for s in range(7):
        col_total = col_total + cols_z[s]
    cols_all[y] = col_total
    cols_s3 = [send(cols_all.at[y], cols_all.at[y], on_y(s)) for s in (1, 2, 3)]
    arrived(depth_s2)
    depth_all[c, x] = depth_one[...] + depth_y[0] + depth_y[1] + depth_y[2]
    depth_s3 = [send(depth_all.at[c, x], depth_all.at[c, x], on_x(s)) for s in (1, 2, 3)]
    arrived(rows_s2)
    row_total = rows_t[pl.ds(pl.multiple_of(z * 16, 16), 16), :]
    for s in range(7):
        row_total = row_total + rows_z[s]
    rows_out[...] = row_total[:, :64]

    own = pl.ds(pl.multiple_of(z * 8, 8), 8)
    arrived(core_z)
    total = tile_sum[own, :]
    for s in range(7):
        total = total + tile_in[s]
    tile_all[own, :] = total
    core_g = [send(tile_all.at[own, :], tile_all.at[own, :], on_z(s)) for s in range(1, 8)]
    arrived(depth_s3)
    depth_s4 = send(depth_all.at[c], depth_all.at[c], mate())
    arrived(core_g)
    turned = jnp.concatenate([tile_all[...], jnp.zeros((64, 128), f32)], axis=0).T
    core_all[c, x, y] = turned[:64] + pltpu.roll(turned[64:], 64, axis=1)

    def pass_low(block_y):
        block = core_all.at[c, x, block_y, low]
        return [send(block, block, on_x(s)) for s in far_first]

    def pass_high(block_x):
        block = core_all.at[c, block_x, y, high]
        return [send(block, block, on_y(s)) for s in far_first]

    kept, handed = [], []

    def hand(*where):
        piece, place_out = core_all.at[where], core_out.at[where]
        handed.append(send(piece, place_out, mate()))
        kept.append(fetch(piece, place_out, local_sem.at[4 + len(kept)]))

    own_low = core_all.at[c, x, y, low]
    own_high = core_all.at[c, x, y, high]
    back_y0 = {s: send(own_low, own_low, on_y(s)) for s in far_first}
    back_x1 = {s: send(own_high, own_high, on_x(s)) for s in far_first}
    back_x0 = [pass_low(y)]
    back_y1 = [pass_high(x)]
    for s in (1, 3, 2):
        back_y0[s].wait_recv()
        back_x0.append(pass_low((y + 4 - s) % 4))
        back_x1[s].wait_recv()
        back_y1.append(pass_high((x + 4 - s) % 4))
    hand(c, x, slice(None), low)
    hand(c, slice(None), y, high)

    arrived(cols_s3)
    whole = cols_all[...].reshape(64, 128)
    cols_out[...] = jnp.where(z % 2 == 1, pltpu.roll(whole, 64, axis=1), whole)[:, :64]

    for place_at, s in ((1, 1), (2, 3), (0, 2)):
        arrived([blocks[place_at] for blocks in back_x0])
        hand(c, (x + 4 - s) % 4, slice(None), low)
        arrived([blocks[place_at] for blocks in back_y1])
        hand(c, slice(None), (y + 4 - s) % 4, high)
    depth_s4.wait_recv()
    depth_out[...] = depth_all[...].reshape(64, 128)
    assert len(started) == send_sem.shape[0] == recv_sem.shape[0]
    arrived(handed)
    for copy in kept:
        copy.wait()
    for copy in started:
        copy.wait_send()


MIDDLE = 4


def tucker_gradients(coords, counts, rows, cols, depth, core, data, weights):
    vmem = pl.BlockSpec(memory_space=pltpu.VMEM)
    smem = pl.BlockSpec(memory_space=pltpu.SMEM)
    hbm = pl.BlockSpec(memory_space=pltpu.HBM)
    slots = data.shape[0]
    copies = 142

    def buf(*shape):
        return pltpu.VMEM(shape, f32)

    def buf16(*shape):
        return pltpu.VMEM(shape, bf16)

    return pl.pallas_call(
        tucker_kernel,
        out_shape=(
            jax.ShapeDtypeStruct((2, 4, 4, 64, 128), f32),
            jax.ShapeDtypeStruct((16, 64), f32),
            jax.ShapeDtypeStruct((64, 64), f32),
            jax.ShapeDtypeStruct((64, 128), f32),
        ),
        in_specs=[smem, smem] + [hbm] * 6,
        out_specs=(hbm, vmem, vmem, vmem),
        scratch_shapes=[
            buf16(16, 64),
            buf16(64, 64),
            buf16(64, 128),
            buf16(64, 64, 64),
            buf16(slots, 128, 32, 128),
            buf16(slots, 128, 32, 128),
            buf16(8, 8, 8, 128),
            buf16(8, 32, 128),
            buf(8, 16, 64),
            buf(64 * 65, 128),
            buf16(64, 64, 128),
            buf(128 * 17, 128),
            buf(slots * 16 * 65, 128),
            buf(2, 4, 4, 64, 128),
            buf(4, 2, 64, 128),
            buf(4, 64, 128),
            buf(2, 4, 8, 128),
            buf(4, 4, 64, 128),
            buf(4, 4, 64, 128),
            buf(3, 4, 32, 128),
            buf(3, 4, 32, 128),
            buf(4, 32, 128),
            buf(4, 32, 128),
            buf(3, 32, 128),
            buf(3, 32, 128),
            buf(64, 128),
            buf(7, 8, 128),
            buf(64, 128),
            buf(2, 4, 4, 64, 128),
            buf(4, 64, 128),
            buf(4, 64, 128),
            buf(3, 64, 128),
            buf(128, 128),
            buf(7, 16, 128),
            buf(3, 4, 16, 128),
            buf(4, 16, 128),
            buf(7, 16, 128),
            buf(4, 16, 128),
            buf(4, 8, 128),
            buf(4, 8, 128),
            buf(3, 8, 128),
            buf(8, 128),
            buf(3, 8, 128),
            buf(2, 4, 8, 128),
            pltpu.SemaphoreType.DMA((copies,)),
            pltpu.SemaphoreType.DMA((copies,)),
            pltpu.SemaphoreType.DMA((12,)),
            pltpu.SemaphoreType.DMA((slots,)),
            pltpu.SemaphoreType.DMA((slots,)),
        ],
        compiler_params=pltpu.CompilerParams(
            collective_id=0, has_side_effects=True, vmem_limit_bytes=67043328
        ),
        name="tucker_gradients",
    )(coords, counts, rows, cols, depth, core, data, weights)


def unpack_kernel(core_ref, rows_ref, cols_ref, depth_ref, core_out, rows_out, cols_out, depth_out):
    core_out[0] = core_ref[:, :, :64]
    core_out[1] = core_ref[:, :, 64:]

    @pl.when(pl.program_id(0) == 0)
    def _():
        rows_out[...] = rows_ref[...]
        cols_out[...] = cols_ref[...]
        depth_out[...] = depth_ref[...]


def unpack_results(core, rows, cols, depth):
    steps = 2
    part = core.shape[0] // steps

    def whole(value):
        return pl.BlockSpec(value.shape, lambda step: (0, 0))

    return pl.pallas_call(
        unpack_kernel,
        out_shape=(
            jax.ShapeDtypeStruct((2, 32, 64, 64), f32),
            jax.ShapeDtypeStruct(rows.shape, f32),
            jax.ShapeDtypeStruct(cols.shape, f32),
            jax.ShapeDtypeStruct(depth.shape, f32),
        ),
        grid=(steps,),
        in_specs=[
            pl.BlockSpec((part, 64, 128), lambda step: (step, 0, 0)),
            whole(rows), whole(cols), whole(depth),
        ],
        out_specs=(
            pl.BlockSpec((2, part, 64, 64), lambda step: (0, step, 0, 0)),
            whole(rows), whole(cols), whole(depth),
        ),
        compiler_params=pltpu.CompilerParams(dimension_semantics=("arbitrary",), vmem_limit_bytes=67043328),
        name="unpack_results",
    )(core, rows, cols, depth)


def on_device(
    observed, weights, coords, counts, factor_rows, factor_cols, factor_depth, core_tensor
):
    core, rows_gradient, cols_gradient, depth_gradient = tucker_gradients(
        coords.transpose(0, 3, 1, 2), counts, factor_rows.T, factor_cols, factor_depth, core_tensor,
        observed.reshape(observed.shape[2:]), weights.reshape(weights.shape[2:]),
    )
    core, rows_gradient, cols_gradient, depth_gradient = unpack_results(
        core.reshape(32, 64, 128), rows_gradient, cols_gradient, depth_gradient
    )
    return (rows_gradient.T, cols_gradient, depth_gradient, core.reshape(64, 64, 64))


def solution(mesh):
    in_specs = (
        P("ia", "ja", "ka", None, None, None),
        P("ia", "ja", "ka", None, None, None),
        P("ia", "ja", "ka", None),
        P("ia", "ja", "ka"),
        P(None, ("ia", "ja", "ka")),
        P(None, ("ja", "ka")),
        P(),
        P(),
    )
    out_specs = (P(None, ("ia", "ja", "ka")), P(None, ("ja", "ka")), P(None, "ka"), P())
    return jax.shard_map(
        on_device, mesh=mesh, in_specs=in_specs, out_specs=out_specs, check_vma=False
    )
```

```python
import jax
import jax.numpy as jnp
from jax import lax
from jax.experimental import pallas as pl
from jax.experimental.pallas import tpu as pltpu
from jax.sharding import PartitionSpec as P

MESH = pl.DeviceIdType.MESH
f32 = jnp.float32
bf16 = jnp.bfloat16
resid_scale = 1.0 / 64.0

NN = (((1,), (0,)), ((), ()))
NT = (((1,), (1,)), ((), ()))
TN = (((0,), (0,)), ((), ()))


def dot(a, b, dims=NN):
    return lax.dot_general(a, b, dims, preferred_element_type=f32)


def low_lanes(shape):
    return lax.broadcasted_iota(jnp.int32, shape, len(shape) - 1) < 64


def unit(size):
    return (
        lax.broadcasted_iota(jnp.int32, (size, size), 0)
        == lax.broadcasted_iota(jnp.int32, (size, size), 1)
    ).astype(bf16)


def twice(value, axis):
    return jnp.concatenate([value, value], axis=axis)


def same(a, b):
    return (1 - jnp.minimum((a - b) * (a - b), 1)).astype(f32)


def split_terms(value):
    lead = value.astype(bf16)
    return lead, (value - lead.astype(f32)).astype(bf16)


def tucker_kernel(
    coords, counts, rows_hbm, cols_hbm, depth_hbm, core_hbm, data_hbm, weight_hbm,
    core_out, rows_out, cols_out, depth_out,
    rows_in, cols_in, slab_in, core_in, data_in, weight_in,
    row_buf, col_buf, slab_buf, first_wide, first_buf, mid, back_buf, core_own, rows_own_sum, cols_own_sum, depth_own,
    core_pair, core_sum, core_x, core_y, half_x, half_y, end_y, end_x, tile_sum, tile_in, tile_all, core_all,
    rows_pair, rows_sum, rows_x, rows_t, rows_z,
    cols_y, cols_sum, cols_z, cols_all,
    depth_pair, depth_sum, depth_x, depth_one, depth_y, depth_all,
    send_sem, recv_sem, local_sem, data_sem, weight_sem,
):
    y = lax.axis_index("ia")
    ja = lax.axis_index("ja")
    z = lax.axis_index("ka")
    x = ja // 2
    c = ja % 2
    o = 1 - c
    low = pl.ds(0, 32)
    high = pl.ds(32, 32)

    def fetch(src, dst, sem):
        copy = pltpu.make_async_copy(src, dst, sem)
        copy.start()
        return copy

    rows_copy = fetch(rows_hbm, rows_in, local_sem.at[0])
    cols_copy = fetch(cols_hbm, cols_in, local_sem.at[1])
    slab_copy = fetch(
        depth_hbm.at[:, pl.ds(pl.multiple_of(z * 128, 128), 128)], slab_in, local_sem.at[2]
    )
    core_copy = fetch(core_hbm, core_in, local_sem.at[3])

    def mate():
        return {"ja": x * 2 + o}

    def on_ja(step):
        return {"ja": (ja + step) % 8}

    def on_x(step):
        return {"ja": ((x + step) % 4) * 2 + c}

    def on_y(step):
        return {"ia": (y + step) % 4}

    def on_z(step):
        return {"ka": (z + step) % 8}

    barrier = pltpu.get_barrier_semaphore()
    targets = [on_z(s) for s in range(1, 8)] + [on_ja(s) for s in range(1, 8)] + [on_y(s) for s in (1, 2, 3)]
    for target in targets:
        pl.semaphore_signal(barrier, inc=1, device_id=target, device_id_type=MESH)

    slots = data_hbm.shape[0]
    for slot in range(slots):
        fetch(data_hbm.at[slot], data_in.at[slot], data_sem.at[slot])
        fetch(weight_hbm.at[slot], weight_in.at[slot], weight_sem.at[slot])

    started = []

    def send(src, dst, target):
        slot = len(started)
        copy = pltpu.make_async_remote_copy(
            src_ref=src, dst_ref=dst, send_sem=send_sem.at[slot], recv_sem=recv_sem.at[slot],
            device_id=target, device_id_type=MESH,
        )
        copy.start()
        started.append(copy)
        return copy

    def arrived(copies):
        for copy in copies:
            copy.wait_recv()

    rows_copy.wait()
    own_rows = dot(rows_in[...], twice(unit(64), 1))
    row_buf[ja, z] = jnp.where(low_lanes((8, 128)), own_rows[:8], own_rows[8:]).astype(bf16)
    cols_copy.wait()
    own_cols = dot(unit(64), twice(cols_in[...], 0), NT)
    col_buf[z] = jnp.where(low_lanes((32, 128)), own_cols[:32], own_cols[32:]).astype(bf16)
    pl.semaphore_wait(barrier, len(targets))
    order = (4, 3, 5, 2, 6, 1, 7)
    deep_rows = [send(row_buf.at[ja, z], row_buf.at[ja, z], on_z(s)) for s in order]
    deep_cols = [send(col_buf.at[z], col_buf.at[z], on_z(s)) for s in order]

    slab_copy.wait()
    slab_turned = dot(unit(128), slab_in[...], NT)
    slab_buf[...] = slab_turned.reshape(8, 16, 64)
    slab_rows = jnp.concatenate(
        [slab_turned[t * 32 + half * 16 : t * 32 + half * 16 + 16] for half in range(2) for t in range(4)], axis=0
    ).astype(bf16)
    core_copy.wait()

    def first_of(pair, carry):
        left = core_in[pair * 2]
        right = core_in[pair * 2 + 1]
        both = dot(slab_rows, jnp.concatenate([left, left, right, right], axis=0), NT)
        for side in range(2):
            piece = both[:, side * 128 : side * 128 + 128]
            first_wide[pl.ds(pair * 2 + side, 64, stride=65), :] = jnp.where(
                low_lanes((64, 128)), piece[:64], piece[64:]
            )
        return carry

    lax.fori_loop(0, 32, first_of, 0, unroll=4)

    arrived(deep_rows)
    wide_rows = [send(row_buf.at[ja], row_buf.at[ja], on_ja(s)) for s in order]

    def round_of(step, carry):
        first_buf[step] = first_wide[pl.ds(step * 65, 64), :].astype(bf16)
        return carry

    lax.fori_loop(0, 64, round_of, 0, unroll=8)
    rows_own_sum[...] = jnp.zeros_like(rows_own_sum)
    cols_own_sum[...] = jnp.zeros_like(cols_own_sum)
    arrived(deep_cols)
    arrived(wide_rows)

    live_count = counts[0, 0, 0]

    def place(slot):
        p = coords[0, 0, 0, slot] & 7
        q = coords[0, 1, 0, slot] & 3
        t = coords[0, 2, 0, slot] & 3
        return p, q, t

    def one_slot(slot, carry):
        p, q, t = place(slot)
        alive = jnp.clip(live_count - slot, 0, 1).astype(f32)
        packed_rows = row_buf[p].astype(f32).reshape(64, 128)
        turned_rows = pltpu.roll(packed_rows, 64, axis=1)
        row_t = jnp.concatenate(
            [part[s * 8 : s * 8 + 8] for s in range(8) for part in (packed_rows, turned_rows)], axis=0
        )[:, :64].astype(bf16)
        row_n = (dot(unit(64), row_t, NT) * alive).astype(bf16)
        row_n2 = twice(row_n, 1)
        packed_cols = jnp.concatenate([col_buf[q * 2], col_buf[q * 2 + 1]], axis=0).astype(f32)
        turned_cols = pltpu.roll(packed_cols, 64, axis=1)
        left = low_lanes((64, 128))
        first_half = jnp.where(left, packed_cols, turned_cols)
        second_half = jnp.where(left, turned_cols, packed_cols)
        col_t = jnp.concatenate(
            [first_half[:32], second_half[:32], first_half[32:], second_half[32:]], axis=0
        )
        left = low_lanes((128, 128))
        zero = jnp.zeros((128, 128), f32)
        col_low = jnp.where(left, col_t, zero)
        col_high = jnp.where(left, zero, col_t)
        to_model = jnp.concatenate([twice(col_low, 1), twice(col_high, 1)], axis=0).astype(bf16)
        to_back = (jnp.concatenate([col_low, col_high], axis=0) * resid_scale).astype(bf16)

        def forward(pair, carry):
            kk = pair * 2
            part = dot(
                row_t, jnp.concatenate([first_buf[t * 16 + kk], first_buf[t * 16 + kk + 1]], axis=1)
            )
            mid[pl.ds(kk, 128, stride=17), :] = part[:, :128]
            mid[pl.ds(kk + 1, 128, stride=17), :] = part[:, 128:]
            return carry

        lax.fori_loop(0, 8, forward, 0, unroll=8)
        pltpu.make_async_copy(data_hbm.at[slot], data_in.at[slot], data_sem.at[slot]).wait()
        pltpu.make_async_copy(weight_hbm.at[slot], weight_in.at[slot], weight_sem.at[slot]).wait()

        def middle(step, col_part):
            base = step * 16
            lead, rest = split_terms(
                jnp.concatenate([mid[pl.ds((base + i) * 17, 16), :] for i in range(16)], axis=0)
            )
            model = dot(jnp.concatenate([lead, rest], axis=1), to_model, NT)

            def half_of(half):
                at = (slot, pl.ds(base, 16), pl.ds(half * 16, 16), slice(None))
                data = data_in[at].reshape(256, 128).astype(f32)
                weight = weight_in[at].reshape(256, 128).astype(f32)
                return (weight * (model[:, half * 128 : half * 128 + 128] - data)).astype(bf16)

            residual = jnp.concatenate([half_of(0), half_of(1)], axis=1)
            back = dot(residual, to_back)
            for i in range(16):
                mid[pl.ds((base + i) * 17, 16), :] = back[i * 16 : i * 16 + 16]
            return col_part + dot(lead, residual, TN)

        col_part = lax.fori_loop(0, 8, middle, jnp.zeros((128, 256), f32), unroll=MIDDLE)
        col_part = (col_part[:64, :128] + col_part[64:, 128:]) * resid_scale
        for part in range(4):
            cols_own_sum[part] += col_part * (same(q, part) * alive)

        def backward(kk, row_part):
            lead, rest = split_terms(mid[pl.ds(kk, 128, stride=17), :])
            both = dot(row_n2, jnp.concatenate([lead, rest], axis=0))
            back_buf[pl.ds((slot * 16 + kk) * 65, 64), :] = both.astype(bf16).astype(f32)
            return row_part + dot(
                twice(first_buf[t * 16 + kk], 1), jnp.concatenate([lead, rest], axis=1), NT
            )

        row_part = lax.fori_loop(0, 16, backward, jnp.zeros((64, 128), f32), unroll=16)
        for part in range(8):
            rows_own_sum[part // 2, part % 2] += row_part * (same(p, part) * alive)
        return carry

    lax.fori_loop(0, slots, one_slot, 0)

    rows_c = send(rows_own_sum.at[:, o], rows_pair, mate())
    cols_s1 = [
        send(cols_own_sum.at[:, pl.ds(pl.multiple_of(((y + s) % 4) * 16, 16), 16), :], cols_y.at[s - 1], on_y(s))
        for s in (1, 2, 3)
    ]

    slab_slots = jnp.concatenate(
        [
            slab_buf[place(slot)[2] * 2 + half]
            for half in range(2)
            for slot in range(slots)
        ],
        axis=0,
    ).astype(bf16)
    slab_n = dot(unit(64), slab_slots, NT).astype(bf16)
    tall = slots * 16
    left_tall = low_lanes((tall, 128))

    def finish_group(half, group, depth_part):
        def finish(step, depth_part):
            u = half * 16 + group * 4 + step
            one = back_buf[pl.ds(u, tall, stride=65), :]
            two = back_buf[pl.ds(u + 32, tall, stride=65), :]
            both = jnp.concatenate(
                [
                    jnp.where(left_tall, one, pltpu.roll(two, 64, axis=1)),
                    jnp.where(left_tall, pltpu.roll(one, 64, axis=1), two),
                ],
                axis=0,
            ).astype(bf16)
            core_own[half, group, step] = dot(slab_n, both)
            piece = jnp.concatenate([core_in[u], core_in[u + 32]], axis=0)
            return depth_part + dot(both, piece)

        return lax.fori_loop(0, 4, finish, depth_part, unroll=4)

    depth_part = jnp.zeros((2 * tall, 64), f32)
    core_c = []
    for group in range(4):
        depth_part = finish_group(o, group, depth_part)
        core_c.append(send(core_own.at[o, group], core_pair.at[group], mate()))
    rows_c.wait_recv()
    rows_sum[...] = rows_own_sum[:, c] + rows_pair[...]
    rows_s1 = [send(rows_sum.at[(x + s) % 4], rows_x.at[s - 1], on_x(s)) for s in (1, 2, 3)]
    for group in range(4):
        depth_part = finish_group(c, group, depth_part)

    for group in range(4):
        core_c[group].wait_recv()
        core_sum[group] = core_own[c, group] + core_pair[group]
    far_first = (2, 1, 3)
    core_x0, core_y1 = {}, {}
    for other in (2, 1, 3, 0):
        at_y = (y + other) % 4
        at_x = (x + other) % 4
        core_x0[other] = [
            send(core_sum.at[(x + s) % 4, at_y, low], core_x.at[s - 1, at_y], on_x(s)) for s in far_first
        ]
        core_y1[other] = [
            send(core_sum.at[at_x, (y + s) % 4, high], core_y.at[s - 1, at_x], on_y(s)) for s in far_first
        ]
    depth_pieces = []
    for t in range(4):
        for half in range(2):
            piece = jnp.zeros((16, 64), f32)
            for slot in range(slots):
                at = half * tall + slot * 16
                piece = piece + depth_part[at : at + 16] * same(place(slot)[2], t)
            depth_pieces.append(piece)
    depth_turned = jnp.concatenate(
        [jnp.concatenate(depth_pieces, axis=0), jnp.zeros((128, 64), f32)], axis=1
    ).T[:64]
    depth_own[...] = depth_turned.reshape(2, 4, 8, 128)
    depth_c = send(depth_own.at[o], depth_pair, mate())

    arrived(cols_s1)
    cols_sum[...] = (
        cols_own_sum[:, pl.ds(pl.multiple_of(y * 16, 16), 16), :] + cols_y[0] + cols_y[1] + cols_y[2]
    )
    cols_s2 = [send(cols_sum.at[((z + s) % 8) // 2], cols_z.at[s - 1], on_z(s)) for s in range(1, 8)]

    core_y0, core_x1 = [], []
    for other in (2, 1, 3, 0):
        at_y = (y + other) % 4
        at_x = (x + other) % 4
        arrived(core_x0[other])
        half_x[at_y] = core_sum[x, at_y, low] + core_x[0, at_y] + core_x[1, at_y] + core_x[2, at_y]
        if other:
            core_y0.append(send(half_x.at[at_y], end_y.at[other - 1], on_y(other)))
        arrived(core_y1[other])
        half_y[at_x] = core_sum[at_x, y, high] + core_y[0, at_x] + core_y[1, at_x] + core_y[2, at_x]
        if other:
            core_x1.append(send(half_y.at[at_x], end_x.at[other - 1], on_x(other)))

    depth_c.wait_recv()
    depth_sum[...] = depth_own[c] + depth_pair[...]
    depth_s1 = [send(depth_sum.at[(x + s) % 4], depth_x.at[s - 1], on_x(s)) for s in (1, 2, 3)]
    arrived(rows_s1)
    rows_own = rows_sum[x] + rows_x[0] + rows_x[1] + rows_x[2]
    rows_t[...] = jnp.concatenate([rows_own, jnp.zeros((64, 128), f32)], axis=0).T
    rows_s2 = [
        send(rows_t.at[pl.ds(pl.multiple_of(((z + s) % 8) * 16, 16), 16), :], rows_z.at[s - 1], on_z(s))
        for s in range(1, 8)
    ]
    arrived(depth_s1)
    depth_one[...] = depth_sum[x] + depth_x[0] + depth_x[1] + depth_x[2]
    depth_s2 = [send(depth_one, depth_y.at[s - 1], on_y(s)) for s in (1, 2, 3)]

    arrived(core_y0)
    tile_sum[low] = half_x[y] + end_y[0] + end_y[1] + end_y[2]
    arrived(core_x1)
    tile_sum[high] = half_y[x] + end_x[0] + end_x[1] + end_x[2]
    core_z = [
        send(tile_sum.at[pl.ds(pl.multiple_of(((z + s) % 8) * 8, 8), 8), :], tile_in.at[s - 1], on_z(s))
        for s in range(1, 8)
    ]

    arrived(cols_s2)
    col_total = cols_sum[z // 2]
    for s in range(7):
        col_total = col_total + cols_z[s]
    cols_all[y] = col_total
    cols_s3 = [send(cols_all.at[y], cols_all.at[y], on_y(s)) for s in (1, 2, 3)]
    arrived(depth_s2)
    depth_all[c, x] = depth_one[...] + depth_y[0] + depth_y[1] + depth_y[2]
    depth_s3 = [send(depth_all.at[c, x], depth_all.at[c, x], on_x(s)) for s in (1, 2, 3)]
    arrived(rows_s2)
    row_total = rows_t[pl.ds(pl.multiple_of(z * 16, 16), 16), :]
    for s in range(7):
        row_total = row_total + rows_z[s]
    rows_out[...] = row_total[:, :64]

    own = pl.ds(pl.multiple_of(z * 8, 8), 8)
    arrived(core_z)
    total = tile_sum[own, :]
    for s in range(7):
        total = total + tile_in[s]
    tile_all[own, :] = total
    core_g = [send(tile_all.at[own, :], tile_all.at[own, :], on_z(s)) for s in range(1, 8)]
    arrived(depth_s3)
    depth_s4 = send(depth_all.at[c], depth_all.at[c], mate())
    arrived(core_g)
    turned = jnp.concatenate([tile_all[...], jnp.zeros((64, 128), f32)], axis=0).T
    core_all[c, x, y] = turned[:64] + pltpu.roll(turned[64:], 64, axis=1)

    def pass_low(block_y):
        block = core_all.at[c, x, block_y, low]
        return [send(block, block, on_x(s)) for s in far_first]

    def pass_high(block_x):
        block = core_all.at[c, block_x, y, high]
        return [send(block, block, on_y(s)) for s in far_first]

    kept, handed = [], []

    def hand(*where):
        piece, place_out = core_all.at[where], core_out.at[where]
        handed.append(send(piece, place_out, mate()))
        kept.append(fetch(piece, place_out, local_sem.at[4 + len(kept)]))

    own_low = core_all.at[c, x, y, low]
    own_high = core_all.at[c, x, y, high]
    back_y0 = {s: send(own_low, own_low, on_y(s)) for s in far_first}
    back_x1 = {s: send(own_high, own_high, on_x(s)) for s in far_first}
    back_x0 = [pass_low(y)]
    back_y1 = [pass_high(x)]
    for s in (1, 3, 2):
        back_y0[s].wait_recv()
        back_x0.append(pass_low((y + 4 - s) % 4))
        back_x1[s].wait_recv()
        back_y1.append(pass_high((x + 4 - s) % 4))
    hand(c, x, slice(None), low)
    hand(c, slice(None), y, high)

    arrived(cols_s3)
    whole = cols_all[...].reshape(64, 128)
    cols_out[...] = jnp.where(z % 2 == 1, pltpu.roll(whole, 64, axis=1), whole)[:, :64]

    for place_at, s in ((1, 1), (2, 3), (0, 2)):
        arrived([blocks[place_at] for blocks in back_x0])
        hand(c, (x + 4 - s) % 4, slice(None), low)
        arrived([blocks[place_at] for blocks in back_y1])
        hand(c, slice(None), (y + 4 - s) % 4, high)
    depth_s4.wait_recv()
    depth_out[...] = depth_all[...].reshape(64, 128)
    assert len(started) == send_sem.shape[0] == recv_sem.shape[0]
    arrived(handed)
    for copy in kept:
        copy.wait()
    for copy in started:
        copy.wait_send()


MIDDLE = 4


def tucker_gradients(coords, counts, rows, cols, depth, core, data, weights):
    vmem = pl.BlockSpec(memory_space=pltpu.VMEM)
    smem = pl.BlockSpec(memory_space=pltpu.SMEM)
    hbm = pl.BlockSpec(memory_space=pltpu.HBM)
    slots = data.shape[0]
    copies = 142

    def buf(*shape):
        return pltpu.VMEM(shape, f32)

    def buf16(*shape):
        return pltpu.VMEM(shape, bf16)

    return pl.pallas_call(
        tucker_kernel,
        out_shape=(
            jax.ShapeDtypeStruct((2, 4, 4, 64, 128), f32),
            jax.ShapeDtypeStruct((16, 64), f32),
            jax.ShapeDtypeStruct((64, 64), f32),
            jax.ShapeDtypeStruct((64, 128), f32),
        ),
        in_specs=[smem, smem] + [hbm] * 6,
        out_specs=(hbm, vmem, vmem, vmem),
        scratch_shapes=[
            buf16(16, 64),
            buf16(64, 64),
            buf16(64, 128),
            buf16(64, 64, 64),
            buf16(slots, 128, 32, 128),
            buf16(slots, 128, 32, 128),
            buf16(8, 8, 8, 128),
            buf16(8, 32, 128),
            buf(8, 16, 64),
            buf(64 * 65, 128),
            buf16(64, 64, 128),
            buf(128 * 17, 128),
            buf(slots * 16 * 65, 128),
            buf(2, 4, 4, 64, 128),
            buf(4, 2, 64, 128),
            buf(4, 64, 128),
            buf(2, 4, 8, 128),
            buf(4, 4, 64, 128),
            buf(4, 4, 64, 128),
            buf(3, 4, 32, 128),
            buf(3, 4, 32, 128),
            buf(4, 32, 128),
            buf(4, 32, 128),
            buf(3, 32, 128),
            buf(3, 32, 128),
            buf(64, 128),
            buf(7, 8, 128),
            buf(64, 128),
            buf(2, 4, 4, 64, 128),
            buf(4, 64, 128),
            buf(4, 64, 128),
            buf(3, 64, 128),
            buf(128, 128),
            buf(7, 16, 128),
            buf(3, 4, 16, 128),
            buf(4, 16, 128),
            buf(7, 16, 128),
            buf(4, 16, 128),
            buf(4, 8, 128),
            buf(4, 8, 128),
            buf(3, 8, 128),
            buf(8, 128),
            buf(3, 8, 128),
            buf(2, 4, 8, 128),
            pltpu.SemaphoreType.DMA((copies,)),
            pltpu.SemaphoreType.DMA((copies,)),
            pltpu.SemaphoreType.DMA((12,)),
            pltpu.SemaphoreType.DMA((slots,)),
            pltpu.SemaphoreType.DMA((slots,)),
        ],
        compiler_params=pltpu.CompilerParams(
            collective_id=0, has_side_effects=True, vmem_limit_bytes=67043328
        ),
        name="tucker_gradients",
    )(coords, counts, rows, cols, depth, core, data, weights)


def unpack_kernel(core_ref, rows_ref, cols_ref, depth_ref, core_out, rows_out, cols_out, depth_out):
    core_out[0] = core_ref[:, :, :64]
    core_out[1] = core_ref[:, :, 64:]

    @pl.when(pl.program_id(0) == 0)
    def _():
        rows_out[...] = rows_ref[...]
        cols_out[...] = cols_ref[...]
        depth_out[...] = depth_ref[...]


def unpack_results(core, rows, cols, depth):
    steps = 2
    part = core.shape[0] // steps

    def whole(value):
        return pl.BlockSpec(value.shape, lambda step: (0, 0))

    return pl.pallas_call(
        unpack_kernel,
        out_shape=(
            jax.ShapeDtypeStruct((2, 32, 64, 64), f32),
            jax.ShapeDtypeStruct(rows.shape, f32),
            jax.ShapeDtypeStruct(cols.shape, f32),
            jax.ShapeDtypeStruct(depth.shape, f32),
        ),
        grid=(steps,),
        in_specs=[
            pl.BlockSpec((part, 64, 128), lambda step: (step, 0, 0)),
            whole(rows), whole(cols), whole(depth),
        ],
        out_specs=(
            pl.BlockSpec((2, part, 64, 64), lambda step: (0, step, 0, 0)),
            whole(rows), whole(cols), whole(depth),
        ),
        compiler_params=pltpu.CompilerParams(dimension_semantics=("arbitrary",), vmem_limit_bytes=67043328),
        name="unpack_results",
    )(core, rows, cols, depth)


def on_device(
    observed, weights, coords, counts, factor_rows, factor_cols, factor_depth, core_tensor
):
    core, rows_gradient, cols_gradient, depth_gradient = tucker_gradients(
        coords.transpose(0, 3, 1, 2), counts, factor_rows.T, factor_cols, factor_depth, core_tensor,
        observed.reshape(observed.shape[2:]), weights.reshape(weights.shape[2:]),
    )
    core, rows_gradient, cols_gradient, depth_gradient = unpack_results(
        core.reshape(32, 64, 128), rows_gradient, cols_gradient, depth_gradient
    )
    return (rows_gradient.T, cols_gradient, depth_gradient, core.reshape(64, 64, 64))


def solution(mesh):
    in_specs = (
        P("ia", "ja", "ka", None, None, None),
        P("ia", "ja", "ka", None, None, None),
        P("ia", "ja", "ka", None),
        P("ia", "ja", "ka"),
        P(None, ("ia", "ja", "ka")),
        P(None, ("ja", "ka")),
        P(),
        P(),
    )
    out_specs = (P(None, ("ia", "ja", "ka")), P(None, ("ja", "ka")), P(None, "ka"), P())
    return jax.shard_map(
        on_device, mesh=mesh, in_specs=in_specs, out_specs=out_specs, check_vma=False
    )
```
